32 devices in a mesh: visit: 8 (over y, x, core), row: 4 (over z).
Axes of the slice: x: 2, y: 2, z: 4, core: 2. Of those that a mesh axis runs over, the one named last changes fastest.
Arguments:
- science: float32 [8, 128, 4096], P('visit', 'row'), may hold values from -8 to 8
- basis_kernels: float32 [9, 21, 21], replicated, may hold values from -0.25 to 0.25
- basis_coeffs: float32 [8, 9], P('visit'), may hold values from -2 to 2
- row_starts: int32 [8, 128], P('visit', 'row'), may hold values from -7 to 1
- row_taps: float32 [8, 8, 128], P('visit', None, 'row'), may hold values from -0.2 to 0.45
- col_offsets: int32 [8], P('visit'), may hold values from 0 to 511
- col_starts: int32 [8, 4096], P('visit'), may hold values from -3 to -2
- col_taps: float32 [8, 8, 4096], P('visit'), may hold values from -0.2 to 0.45
- visit_weights: float32 [8], P('visit'), may hold values from 0.25 to 4
- clip_masks: int32 [8, 128, 4096], P('visit', 'row'), may hold values 0 or 1
- decorrelation: float32 [8, 21, 21], P('visit'), may hold values from -0.25 to 0.25
Outputs:
- decorrelated: float32 [8, 128, 4096], P('visit', 'row')
- template: float32 [128, 4096], P('row', 'visit')
The draws below stay inside these ranges and needn't reach their ends.
Inputs may be any that keep to these rules, and one draw needn't show every extreme that they name: Row i of a visit reads matched rows i + row_starts[v, i] to i + row_starts[v, i] + 7.
All inputs are finite; a program needn't handle non-finite values. No bound on the sum of `clip_masks` on one device may be relied on, other than what follows from the above.
Results may differ from the reference program's by a relative error of at most 0.0003.
Values sent between devices are 32-bit elements; how exact they have to be, the bound alone decides.
A program may use at most 64 MiB of HBM per device.

```python
import math
import jax
import jax.numpy as jnp
from jax import lax

W = 4096
KS = 21
NBASIS = 9
TAPS = 8
DITHER = 512
VISITS = 8
H = 128


def place_ends(entries, own_key, least, top_value):
    place = [jax.random.randint(jax.random.fold_in(own_key, axis), (), 0, length) for axis, length in enumerate(entries.shape)]
    main_axis = entries.shape.index(max(entries.shape))
    neighbour = place[:main_axis] + [(place[main_axis] + 1) % entries.shape[main_axis]] + place[main_axis + 1:]
    return entries.at[tuple(place)].set(least).at[tuple(neighbour)].set(top_value)


def block_levels(key, extent, split, smallest, top_value):
    level = 1.0
    for axis_at, shards_of in split:
        steps = jax.random.uniform(jax.random.fold_in(jax.random.fold_in(key, 6), axis_at), (shards_of,), jnp.float32, smallest / len(split), top_value / len(split))
        level = level * jnp.repeat(jnp.exp(steps), extent[axis_at] // shards_of).reshape((-1,) + (1,) * (len(extent) - 1 - axis_at))
    return level


def gaussian(own_key, dims, width, bound, split=(), kind=jnp.bfloat16):
    level = block_levels(own_key, dims, split, -0.22, 0.18) if split else 1.0
    drawn = jax.random.normal(own_key, dims, jnp.float32) * width * level
    return jnp.minimum(jnp.maximum(drawn, -bound), bound).astype(kind)


def setup_inputs(seed: int = 0) -> dict:
    keys = jax.random.split(jax.random.key(seed), 12)
    return {
        "science": gaussian(keys[0], (VISITS, H, W), 1.0, 8.0, ((0, 8), (1, 4)), jnp.float32),
        "basis_kernels": gaussian(keys[1], (NBASIS, KS, KS), (KS * KS) ** -0.5, 0.25, (), jnp.float32),
        "basis_coeffs": gaussian(keys[2], (VISITS, NBASIS), 0.33, 2.0, ((0, 8),), jnp.float32),
        "row_starts": place_ends(jax.random.randint(keys[3], (VISITS, H), -7, 2), jax.random.fold_in(keys[3], 1), -7, 1).astype(jnp.int32),
        "row_taps": jnp.clip(-0.2 + 0.65 * jax.random.uniform(keys[4], (VISITS, TAPS, H), jnp.float32) ** block_levels(keys[4], (VISITS, TAPS, H), ((0, 8), (2, 4)), -0.2, 0.2), -0.2, 0.45),
        "col_offsets": place_ends(jax.random.randint(keys[5], (VISITS,), 0, DITHER), jax.random.fold_in(keys[5], 1), 0, DITHER - 1).astype(jnp.int32),
        "col_starts": place_ends(jax.random.randint(keys[6], (VISITS, W), -3, -1), jax.random.fold_in(keys[6], 1), -3, (-1) - 1).astype(jnp.int32),
        "col_taps": jnp.clip(-0.2 + 0.65 * jax.random.uniform(keys[7], (VISITS, TAPS, W), jnp.float32) ** block_levels(keys[7], (VISITS, TAPS, W), ((0, 8),), -0.2, 0.2), -0.2, 0.45),
        "visit_weights": jnp.clip(jnp.exp(math.log(4.0) - 2.7725887 * jax.random.uniform(keys[8], (VISITS,), jnp.float32) ** block_levels(keys[8], (VISITS,), ((0, 8),), -0.2, 0.2)), 0.25, 4.0),
        "clip_masks": place_ends((jax.random.randint(keys[9], (VISITS, H, W), 0, 8) < 7).astype(jnp.int32), jax.random.fold_in(keys[9], 1), 0, 1),
        "decorrelation": gaussian(keys[10], (VISITS, KS, KS), (KS * KS) ** -0.5, 0.25, ((0, 8),), jnp.float32),
    }


def correlate(pixels, kernel):
    half_width = KS // 2
    result = lax.conv_general_dilated(pixels[None, None], kernel[None, None], (1, 1), ((half_width, half_width), (half_width, half_width)), precision=lax.Precision.HIGHEST)
    return result[0, 0]


def reference(science, basis_kernels, basis_coeffs, row_starts, row_taps, col_offsets, col_starts, col_taps, visit_weights, clip_masks, decorrelation):
    def warp_visit(operands):
        pixels, mixing, shift_rows, taps_rows, dither, shift_cols, taps_cols, weight_now, mask_now = operands
        kernel = jnp.einsum("b,bij->ij", mixing, basis_kernels, precision=lax.Precision.HIGHEST)
        matched = correlate(pixels, kernel)
        padded = jnp.pad(matched, ((TAPS, TAPS), (0, 0)))
        row_index = jnp.arange(H, dtype=jnp.int32) + shift_rows + TAPS
        rowwarp = jnp.zeros((H, W), jnp.float32)
        for tap_index in range(TAPS):
            rowwarp = rowwarp + taps_rows[tap_index][:, None] * jnp.take(padded, row_index + tap_index, axis=0)
        widened = jnp.pad(rowwarp, ((0, 0), (DITHER + 3, 8)))
        actual_start = jnp.arange(W, dtype=jnp.int32) - dither + shift_cols
        warped = jnp.zeros((H, W), jnp.float32)
        for tap_index in range(TAPS):
            warped = warped + taps_cols[tap_index][None, :] * jnp.take(widened, actual_start + DITHER + 3 + tap_index, axis=1)
        covered = ((actual_start >= 0) & (actual_start <= W - TAPS)).astype(jnp.float32)
        share = weight_now * mask_now.astype(jnp.float32) * covered[None, :]
        return warped, share

    warped, share = lax.map(warp_visit, (science, basis_coeffs, row_starts, row_taps, col_offsets, col_starts, col_taps, visit_weights, clip_masks))
    numerator = jnp.sum(share * warped, axis=0)
    denominator = jnp.sum(share, axis=0)
    template = numerator / jnp.maximum(denominator, 1.0)

    def clean_visit(operands):
        warped_now, kernel_now = operands
        return correlate(warped_now - template, kernel_now)

    decorrelated = lax.map(clean_visit, (warped, decorrelation))
    return decorrelated, template
```

```python
import functools

import jax
import jax.numpy as jnp
from jax import lax
from jax.experimental import pallas as pl
from jax.experimental.pallas import tpu as pltpu
from jax.sharding import PartitionSpec as P

KS = 21
HALF = KS // 2
TAPS = 8
PAD = 128
CHUNK = 512
F32 = jnp.float32
BF16 = jnp.bfloat16
MESH = pl.DeviceIdType.MESH
VMEM = pl.BlockSpec(memory_space=pltpu.VMEM)
HBM = pl.BlockSpec(memory_space=pltpu.HBM)
SMEM = pl.BlockSpec(memory_space=pltpu.SMEM)


def padded_width(columns):
    return -(-(columns + 2 * PAD) // CHUNK) * CHUNK


def split(x):
    high = x.astype(BF16)
    low = (x - high.astype(F32)).astype(BF16)
    return high, low


def toeplitz(kernel_t, c, rows, lead):
    line = jnp.broadcast_to(kernel_t[c : c + 1, :], (rows, 128))
    return pltpu.roll(line, lead, 1, stride=1, stride_axis=0)


def kernel_transposed(kernel, square):
    square[...] = jnp.zeros_like(square)
    square[0:KS, 0:KS] = kernel
    return jnp.transpose(square[...])


def piece(high, low, both, partial, start, group, add=False):
    m = both.shape[0]
    window_h = high[:, start : start + CHUNK + 128]
    window_l = low[:, start : start + CHUNK + 128]
    stack_h = [window_h[:, b : b + CHUNK] for b in range(group)]
    stack_l = [window_l[:, b : b + CHUNK] for b in range(group)]
    stack = jnp.concatenate(stack_h + stack_l + stack_h, axis=0)
    total = jnp.dot(both[...], stack, preferred_element_type=F32)
    if add:
        total = total + partial[0:m, start : start + CHUNK]
    partial[0:m, start : start + CHUNK] = total


def shifted_sum(partial, start, rows, group):
    total = jnp.zeros((rows, CHUNK), F32)
    for a in range(-(-KS // group)):
        window = partial[a * rows : (a + 1) * rows, start : start + CHUNK + 2 * PAD]
        shift = PAD + group * a - HALF
        total = total + window[:, shift : shift + CHUNK]
    return total


def store_split(high, low, row, column, values):
    h, l = split(values)
    high[row : row + values.shape[0], column : column + values.shape[1]] = h
    low[row : row + values.shape[0], column : column + values.shape[1]] = l


def store_both(both, values):
    h, l = split(values)
    k = values.shape[1]
    both[:, 0:k] = h
    both[:, k : 2 * k] = h
    both[:, 2 * k : 3 * k] = l


def pack_pair(packed, source, row, columns):
    quarter = columns // 4
    for q in range(4):
        packed[2 * q : 2 * q + 2, :] = source[row : row + 2, q * quarter : (q + 1) * quarter]


def greet(nv, nr):
    v, r = lax.axis_index("visit"), lax.axis_index("row")
    half = nv // 2
    parity, mine = v % 2, v // 2
    barrier = pltpu.get_barrier_semaphore()

    def hello(a, b):
        pl.semaphore_signal(barrier, inc=1, device_id=(a, b), device_id_type=MESH)

    hello(v + 1 - 2 * parity, r)
    for d in range(1, half):
        hello(2 * ((mine + d) % half) + parity, r)

    @pl.when(r > 0)
    def _():
        hello(v, r - 1)

    @pl.when(r < nr - 1)
    def _():
        hello(v, r + 1)


def greeted(nv, nr):
    r = lax.axis_index("row")
    above, below = (r > 0).astype(jnp.int32), (r < nr - 1).astype(jnp.int32)
    pl.semaphore_wait(pltpu.get_barrier_semaphore(), nv // 2 + above + below)


def remote(src, dst, send, recv, device):
    return pltpu.make_async_remote_copy(
        src_ref=src, dst_ref=dst, send_sem=send, recv_sem=recv, device_id=device, device_id_type=MESH
    )


def pair_start(nv, blocks, landed, sems):
    v, r = lax.axis_index("visit"), lax.axis_index("row")
    half = nv // 2
    parity, mine = v % 2, v // 2
    copies = {}
    for d in list(range(1, half)) + [0]:
        k = (mine + d) % half
        copies[d] = remote(
            blocks.at[2 * k + 1 - parity], landed.at[k], sems.at[0, d], sems.at[1, d], (v + 1 - 2 * parity, r)
        )
        copies[d].start()
    return copies


def scatter_start(nv, blocks, landed, pair_copies, sums, arrived, sems):
    v, r = lax.axis_index("visit"), lax.axis_index("row")
    half = nv // 2
    parity, mine = v % 2, v // 2
    copies = []
    for d in range(1, half):
        k = (mine + d) % half
        pair_copies[d].wait()
        sums[d - 1] = blocks[2 * k + parity] + landed[k]
        copy = remote(sums.at[d - 1], arrived.at[d - 1], sems.at[0, d], sems.at[1, d], (2 * k + parity, r))
        copy.start()
        copies.append(copy)
    return copies


def scatter_finish(nv, blocks, landed, pair_copies, arrived, copies):
    v = lax.axis_index("visit")
    half, mine = nv // 2, v // 2
    pair_copies[0].wait()
    total = blocks[v] + landed[mine]
    for d in range(1, half):
        copies[d - 1].wait()
        total = total + arrived[d - 1]
    return total


def exchange_scratch(nv, rows, width):
    half = nv // 2
    return [
        pltpu.VMEM((half, rows, width), F32),
        pltpu.VMEM((half, rows, width), F32),
        pltpu.VMEM((half, rows, width), F32),
        pltpu.SemaphoreType.DMA((2, half)),
        pltpu.SemaphoreType.DMA((2, half)),
    ]


def whole_kernel(
    nv, nr, science_in, basis_in, coeffs_in, row_starts_in, row_taps_in, offsets, col_starts_in, col_taps_in,
    weights, masks_in, decor_in,
    cleaned, template,
    science, basis, coeffs, row_starts, row_taps, col_starts, col_taps, masks, decor, load_sems,
    shares, numerators, warped, difference, gathered, denominator,
    near_top, near_bottom, packs, pairs_top, pairs_bottom,
    late_top, late_bottom, late_pack_top, late_pack_bottom, late_pair_top, late_pair_bottom,
    square, bands, flat, both, flat_own, own_both, flat_edge, edge_both,
    high, low, second_high, second_low, edge_high, edge_low, partial, shifted, mover,
    d_landed, d_sums, d_arrived, d_pair, d_sum,
    n_landed, n_sums, n_arrived, n_pair, n_sum,
    gather_sems, pass_sems, halo_sems, late_sems,
):
    v, r = lax.axis_index("visit"), lax.axis_index("row")
    rows, columns = science.shape
    width = columns // nv
    half = nv // 2
    parity, mine = v % 2, v // 2
    partner = (v + 1 - 2 * parity, r)
    chunks = packs.shape[1]
    span = columns // chunks
    padded = padded_width(columns)
    depth, group = high.shape[0], 3
    middle = rows + 2 * TAPS

    greet(nv, nr)
    loads = [
        pltpu.make_async_copy(src, dst, load_sems.at[n])
        for n, (src, dst) in enumerate([
            (science_in, science), (col_starts_in, col_starts),
            (masks_in, masks), (coeffs_in, coeffs), (basis_in, basis), (row_starts_in, row_starts),
            (row_taps_in, row_taps), (decor_in, decor), (col_taps_in, col_taps),
        ])
    ]
    for load in loads:
        load.start()
    for load in loads:
        load.wait()
    dither = offsets[0]
    for u in range(nv):
        cols = slice(u * width, (u + 1) * width)
        start = col_starts[:, cols] + (lax.broadcasted_iota(jnp.int32, (1, width), 1) + (u * width - dither))
        covered = jnp.where((start >= 0) & (start <= columns - TAPS), weights[0], 0.0)
        shares[u] = masks[:, cols].astype(F32) * covered

    quarter = span // 4
    for n in range(chunks):
        for q in range(4):
            at = n * span + q * quarter
            packs[0, n, 2 * q : 2 * q + 2, :] = science[16:18, at : at + quarter]
            packs[1, n, 2 * q : 2 * q + 2, :] = science[rows - 18 : rows - 16, at : at + quarter]
    greeted(nv, nr)
    up, down = [], []
    for n in range(chunks):
        cols = slice(n * span, (n + 1) * span)
        up.append(remote(science.at[0:16, cols], near_bottom.at[:, cols], halo_sems.at[0, n], halo_sems.at[1, n], (v, r - 1)))
        up.append(remote(packs.at[0, n], pairs_bottom.at[n], halo_sems.at[2, n], halo_sems.at[3, n], (v, r - 1)))
        down.append(remote(science.at[rows - 16 : rows, cols], near_top.at[:, cols], halo_sems.at[4, n], halo_sems.at[5, n], (v, r + 1)))
        down.append(remote(packs.at[1, n], pairs_top.at[n], halo_sems.at[6, n], halo_sems.at[7, n], (v, r + 1)))

    @pl.when(r > 0)
    def _():
        for copy in up:
            copy.start()

    @pl.when(r < nr - 1)
    def _():
        for copy in down:
            copy.start()

    @pl.when(r == 0)
    def _():
        near_top[...] = jnp.zeros_like(near_top)
        pairs_top[...] = jnp.zeros_like(pairs_top)
        late_top[...] = jnp.zeros_like(late_top)
        late_pair_top[...] = jnp.zeros_like(late_pair_top)

    @pl.when(r == nr - 1)
    def _():
        near_bottom[...] = jnp.zeros_like(near_bottom)
        pairs_bottom[...] = jnp.zeros_like(pairs_bottom)
        late_bottom[...] = jnp.zeros_like(late_bottom)
        late_pair_bottom[...] = jnp.zeros_like(late_pair_bottom)

    weight_pairs = pair_start(nv, shares, d_landed, d_pair)

    kernel = coeffs[0] * basis[0]
    for b in range(1, basis.shape[0]):
        kernel = kernel + coeffs[b] * basis[b]
    kernel_t = kernel_transposed(kernel, square)
    m = lax.broadcasted_iota(jnp.int32, (middle, rows), 0) - TAPS
    i = lax.broadcasted_iota(jnp.int32, (middle, rows), 1)
    tap = m - i - row_starts[...]
    inside = (m + r * rows >= 0) & (m + r * rows < nr * rows)
    mix = jnp.zeros((middle, rows), F32)
    for t in range(TAPS):
        mix = mix + jnp.where((tap == t) & inside, row_taps[t : t + 1, :], 0.0)
    for c in range(KS):
        bands[:, c * 128 : (c + 1) * 128] = toeplitz(kernel_t, c, middle, 6)
    folded = lax.dot_general(
        mix, bands[...], (((0,), (0,)), ((), ())), precision=lax.Precision.HIGHEST, preferred_element_type=F32
    )
    flat[...] = jnp.zeros_like(flat)
    for c in range(KS):
        a, b = c // group, c % group
        flat[a * rows : (a + 1) * rows, b * depth : (b + 1) * depth] = folded[:, c * 128 : c * 128 + depth]
    store_both(both, flat[...])

    weight_sums = scatter_start(nv, shares, d_landed, weight_pairs, d_sums, d_arrived, d_sum)

    kernel_t = kernel_transposed(decor[:, 0, :], square)
    flat_own[...] = jnp.zeros_like(flat_own)
    flat_edge[...] = jnp.zeros_like(flat_edge)
    for c in range(KS):
        band = toeplitz(kernel_t, c, rows, 6)
        a, b = c // 8, c % 8
        here = slice(a * rows, (a + 1) * rows)
        flat_own[here, b * rows : (b + 1) * rows] = band[:, 16 : 16 + rows]
        flat_edge[here, b * 32 : b * 32 + 16] = band[:, 0:16]
        flat_edge[here, b * 32 + 16 : b * 32 + 32] = band[:, 16 + rows : 32 + rows]
    store_both(own_both, flat_own[...])
    store_both(edge_both, flat_edge[...])

    for frame in (high, low, second_high, second_low, edge_high, edge_low):
        frame[...] = jnp.zeros_like(frame)
    shifted[...] = jnp.zeros_like(shifted)

    tiles = jnp.full((rows, width + 384), dither // 128, jnp.int32)
    place = lax.broadcasted_iota(jnp.int32, (256, 128), 0) - lax.broadcasted_iota(jnp.int32, (256, 128), 1)
    mover[...] = jnp.where(place == 128 - dither % 128, 1.0, 0.0).astype(BF16)

    def warp(u):
        start = u * width
        count = width // 128 + 2
        window = shifted[:, start + 384 : start + 768 + width]
        for t in range(1, 4):
            at = start + 384 - 128 * t
            window = jnp.where(tiles == t, shifted[:, at : at + width + 384], window)
        h, l = split(window)
        stack_h = jnp.concatenate([h[:, 128 * j : 128 * j + 256] for j in range(count)], axis=0)
        stack_l = jnp.concatenate([l[:, 128 * j : 128 * j + 256] for j in range(count)], axis=0)
        moved = jnp.dot(stack_h, mover[...], preferred_element_type=F32)
        moved = moved + jnp.dot(stack_l, mover[...], preferred_element_type=F32)
        window = jnp.concatenate([moved[j * rows : (j + 1) * rows] for j in range(count)], axis=1)
        cols = slice(start, start + width)
        early = col_starts[:, cols] == -3
        taps = [col_taps[t : t + 1, cols] for t in range(TAPS)]
        total = jnp.zeros((rows, width), F32)
        for lag in range(TAPS + 1):
            now = taps[lag] if lag < TAPS else jnp.zeros_like(taps[0])
            before = taps[lag - 1] if lag > 0 else jnp.zeros_like(taps[0])
            at = 128 + lag - 3
            total = total + jnp.where(early, now, before) * window[:, at : at + width]
        warped[:, cols] = total
        numerators[u] = shares[u] * total

    def number_pair(k):
        return remote(numerators.at[2 * k + 1 - parity], n_landed.at[k], n_pair.at[0, k], n_pair.at[1, k], partner)

    def number_sum(k, d):
        return remote(n_sums.at[k], n_arrived.at[d], n_sum.at[0, d], n_sum.at[1, d], (2 * k + parity, r))

    def forward(k):
        number_pair(k).wait()
        n_sums[k] = numerators[2 * k + parity] + n_landed[k]
        d = (k - mine + half) % half

        @pl.when(d > 0)
        def _():
            number_sum(k, d).start()

    pieces = padded // CHUNK
    done_pieces, done_sums, done_warps, done_pairs, done_forwards = 0, 0, 0, 0, 0
    for n in range(chunks):
        cols = slice(n * span, (n + 1) * span)

        @pl.when(r > 0)
        def _():
            down[2 * n].wait_recv()
            down[2 * n + 1].wait_recv()

        @pl.when(r < nr - 1)
        def _():
            up[2 * n].wait_recv()
            up[2 * n + 1].wait_recv()

        store_split(high, low, 24, PAD + n * span, science[:, cols])
        top = near_top[:, cols]
        bottom = near_bottom[:, cols]
        store_split(high, low, 8, PAD + n * span, top)
        store_split(high, low, 24 + rows, PAD + n * span, bottom)
        for q in range(4):
            at = PAD + n * span + q * quarter
            store_split(high, low, 6, at, pairs_top[n, 2 * q : 2 * q + 2, :])
            store_split(high, low, 40 + rows, at, pairs_bottom[n, 2 * q : 2 * q + 2, :])
        last = n == chunks - 1
        while done_pieces < pieces and (last or (done_pieces + 1) * CHUNK + group - PAD <= (n + 1) * span):
            piece(high, low, both, partial, done_pieces * CHUNK, group)
            done_pieces += 1
        while done_sums < columns // CHUNK and done_sums + 2 <= done_pieces:
            start = done_sums * CHUNK
            shifted[:, 640 + start : 640 + start + CHUNK] = shifted_sum(partial, start, rows, group)
            done_sums += 1
        while done_warps < nv and (done_sums * CHUNK >= (done_warps + 1) * width + 8 or done_sums * CHUNK == columns):
            warp(done_warps)
            done_warps += 1
            if done_warps % 2 == 0:
                number_pair(done_pairs).start()
                done_pairs += 1
                if done_pairs >= 2:
                    forward(done_forwards)
                    done_forwards += 1
    while done_forwards < half:
        forward(done_forwards)
        done_forwards += 1
    denominator[...] = scatter_finish(nv, shares, d_landed, weight_pairs, d_arrived, weight_sums)

    total = n_sums[mine]
    for d in range(1, half):
        number_sum((mine + d) % half, d).wait()
        total = total + n_arrived[d]
    own = total / jnp.maximum(denominator[...], 1.0)
    template[...] = own
    gathered[v] = own
    sends = []
    for d in range(1, half):
        k = (mine + d) % half
        copy = remote(gathered.at[v], gathered.at[v], gather_sems.at[0, d], gather_sems.at[1, d], (2 * k + parity, r))
        copy.start()
        sends.append(copy)

    def passed(d):
        u = 2 * ((mine + half - d) % half) + parity
        return remote(gathered.at[u], gathered.at[u], pass_sems.at[0, d], pass_sems.at[1, d], partner)

    passes = [passed(d) for d in range(half)]
    passes[0].start()
    ups, downs = [], []

    def subtract(u):
        cols = pl.ds(pl.multiple_of(u * width, width), width)
        at = pl.ds(pl.multiple_of(PAD + u * width, 128), width)
        values = warped[:, cols] - gathered[u]
        difference[:, cols] = values
        h, l = split(values)
        second_high[:, at] = h
        second_low[:, at] = l
        n = len(ups)
        ups.append(remote(difference.at[0:8, cols], late_bottom.at[:, cols], late_sems.at[0, n], late_sems.at[1, n], (v, r - 1)))
        downs.append(
            remote(difference.at[rows - 8 : rows, cols], late_top.at[:, cols], late_sems.at[2, n], late_sems.at[3, n], (v, r + 1))
        )

        @pl.when(r > 0)
        def _():
            ups[-1].start()

        @pl.when(r < nr - 1)
        def _():
            downs[-1].start()

    subtract(v)
    for d in range(half):
        if d > 0:
            sends[d - 1].wait_recv()
            passes[d].start()
            subtract(2 * ((mine + half - d) % half) + parity)
        passes[d].wait_recv()
        subtract(2 * ((mine + half - d) % half) + 1 - parity)
    pack_pair(late_pack_top, difference, 8, columns)
    pack_pair(late_pack_bottom, difference, rows - 10, columns)
    ups.append(remote(late_pack_top, late_pair_bottom, late_sems.at[0, nv], late_sems.at[1, nv], (v, r - 1)))
    downs.append(remote(late_pack_bottom, late_pair_top, late_sems.at[2, nv], late_sems.at[3, nv], (v, r + 1)))

    @pl.when(r > 0)
    def _():
        ups[-1].start()

    @pl.when(r < nr - 1)
    def _():
        downs[-1].start()

    for n in range(pieces):
        piece(second_high, second_low, own_both, partial, n * CHUNK, 8)

    @pl.when(r > 0)
    def _():
        for copy in downs:
            copy.wait_recv()

    @pl.when(r < nr - 1)
    def _():
        for copy in ups:
            copy.wait_recv()

    store_split(edge_high, edge_low, 8, PAD, late_top[...])
    store_split(edge_high, edge_low, 16, PAD, late_bottom[...])
    for q in range(4):
        at = PAD + q * (columns // 4)
        store_split(edge_high, edge_low, 6, at, late_pair_top[2 * q : 2 * q + 2, :])
        store_split(edge_high, edge_low, 24, at, late_pair_bottom[2 * q : 2 * q + 2, :])
    for n in range(pieces):
        piece(edge_high, edge_low, edge_both, partial, n * CHUNK, 8, add=True)
        if n > 0 and n * CHUNK <= columns:
            cleaned[:, (n - 1) * CHUNK : n * CHUNK] = shifted_sum(partial, (n - 1) * CHUNK, rows, 8)

    for copy in sends + passes:
        copy.wait_send()

    @pl.when(r > 0)
    def _():
        for copy in up + ups:
            copy.wait_send()

    @pl.when(r < nr - 1)
    def _():
        for copy in down + downs:
            copy.wait_send()


def hand_over(cleaned, template, cleaned_out, template_out, sems):
    first = pltpu.make_async_copy(cleaned, cleaned_out, sems.at[0])
    second = pltpu.make_async_copy(template, template_out, sems.at[1])
    first.start()
    second.start()
    first.wait()
    second.wait()


def shape(*dims):
    return jax.ShapeDtypeStruct(dims, F32)


def in_hbm(array):
    return pltpu.with_memory_space_constraint(array, pltpu.HBM)


def on_device(
    nv, nr, science, basis_kernels, basis_coeffs, row_starts, row_taps, col_offsets,
    col_starts, col_taps, visit_weights, clip_masks, decorrelation,
):
    pixels = science[0]
    rows, columns = pixels.shape
    width = columns // nv
    half = nv // 2
    chunks = 4
    span = columns // chunks
    padded = padded_width(columns)
    depth, group = 80, 3
    tall = -(-KS // group) * rows
    wide = -(-KS // 8) * rows
    f32 = lambda *dims: pltpu.VMEM(dims, F32)
    bf16 = lambda *dims: pltpu.VMEM(dims, BF16)
    cleaned, template = pl.pallas_call(
        functools.partial(whole_kernel, nv, nr),
        out_shape=(pltpu.VMEM((rows, columns), F32), pltpu.VMEM((rows, width), F32)),
        in_specs=[HBM] * 5 + [SMEM] + [HBM] * 2 + [SMEM] + [HBM] * 2,
        out_specs=(VMEM, VMEM),
        scratch_shapes=[
            f32(rows, columns), f32(*basis_kernels.shape), pltpu.SMEM(basis_coeffs.shape[1:], F32),
            pltpu.VMEM((1, rows), jnp.int32), f32(TAPS, rows),
            pltpu.VMEM((1, columns), jnp.int32), f32(TAPS, columns),
            pltpu.VMEM((rows, columns), jnp.int32), f32(KS, 1, KS), pltpu.SemaphoreType.DMA((9,)),
            f32(nv, rows, width), f32(nv, rows, width), f32(rows, columns), f32(rows, columns),
            f32(nv, rows, width), f32(rows, width),
            f32(16, columns), f32(16, columns), f32(2, chunks, 8, span // 4),
            f32(chunks, 8, span // 4), f32(chunks, 8, span // 4),
            f32(8, columns), f32(8, columns), f32(8, columns // 4), f32(8, columns // 4),
            f32(8, columns // 4), f32(8, columns // 4),
            f32(128, 128), f32(rows + 2 * TAPS, KS * 128),
            f32(tall, group * depth), bf16(tall, 3 * group * depth),
            f32(wide, 8 * rows), bf16(wide, 24 * rows),
            f32(wide, 256), bf16(wide, 768),
            bf16(depth, padded + 128), bf16(depth, padded + 128),
            bf16(rows, padded + 128), bf16(rows, padded + 128),
            bf16(32, padded + 128), bf16(32, padded + 128),
            f32(tall, padded), f32(rows, columns + 1024), bf16(256, 128),
        ] + exchange_scratch(nv, rows, width) + exchange_scratch(nv, rows, width) + [
            pltpu.SemaphoreType.DMA((2, half)),
            pltpu.SemaphoreType.DMA((2, half)),
            pltpu.SemaphoreType.DMA((8, chunks)),
            pltpu.SemaphoreType.DMA((4, nv + 1)),
        ],
        compiler_params=pltpu.CompilerParams(
            collective_id=0, has_side_effects=True, vmem_limit_bytes=28 * 1024 * 1024
        ),
        name="whole",
    )(
        *map(in_hbm, (pixels, basis_kernels, basis_coeffs[0], row_starts, row_taps[0])), col_offsets,
        *map(in_hbm, (col_starts, col_taps[0])), visit_weights,
        *map(in_hbm, (clip_masks[0], jnp.transpose(decorrelation, (1, 0, 2)))),
    )
    cleaned, template = pl.pallas_call(
        hand_over,
        out_shape=(shape(rows, columns), shape(rows, width)),
        in_specs=[VMEM, VMEM],
        out_specs=(HBM, HBM),
        scratch_shapes=[pltpu.SemaphoreType.DMA((2,))],
        compiler_params=pltpu.CompilerParams(vmem_limit_bytes=8 * 1024 * 1024),
        name="hand_over",
    )(cleaned, template)
    return (cleaned[None], template)


def solution(mesh):
    nv, nr = mesh.shape["visit"], mesh.shape["row"]
    return jax.shard_map(
        functools.partial(on_device, nv, nr),
        mesh=mesh,
        in_specs=(
            P("visit", "row", None),
            P(),
            P("visit", None),
            P("visit", "row"),
            P("visit", None, "row"),
            P("visit"),
            P("visit", None),
            P("visit", None, None),
            P("visit"),
            P("visit", "row", None),
            P("visit", None, None),
        ),
        out_specs=(P("visit", "row", None), P("row", "visit")),
        check_vma=False,
    )
```

```python
import functools
import heapq

import jax
import jax.numpy as jnp
from jax import lax
from jax.experimental import pallas as pl
from jax.experimental.pallas import tpu as pltpu
from jax.sharding import PartitionSpec as P

KS = 21
HALF = KS // 2
TAPS = 8
PAD = 128
CHUNK = 512
HALO_PARTS = 8
SUM_PARTS = 8
SHARE_PARTS = 4
F32 = jnp.float32
BF16 = jnp.bfloat16
MESH = pl.DeviceIdType.MESH
VMEM = pl.BlockSpec(memory_space=pltpu.VMEM)
HBM = pl.BlockSpec(memory_space=pltpu.HBM)
SMEM = pl.BlockSpec(memory_space=pltpu.SMEM)


def padded_width(columns):
    return -(-(columns + 2 * PAD) // PAD) * PAD


def split(x):
    high = x.astype(BF16)
    low = (x - high.astype(F32)).astype(BF16)
    return high, low


def toeplitz(kernel_t, c, rows, lead):
    line = jnp.broadcast_to(kernel_t[c : c + 1, :], (rows, 128))
    return pltpu.roll(line, lead, 1, stride=1, stride_axis=0)


def kernel_transposed(kernel, square):
    square[...] = jnp.zeros_like(square)
    square[0:KS, 0:KS] = kernel
    return jnp.transpose(square[...])


def piece(high, low, both, partial, start, end, group):
    m, wide = both.shape[0] // 2, end - start
    window_h = high[:, start : end + 128]
    window_l = low[:, start : end + 128]
    stack_h = jnp.concatenate([window_h[:, b : b + wide] for b in range(group)], axis=0)
    stack_l = jnp.concatenate([window_l[:, b : b + wide] for b in range(group)], axis=0)
    top = jnp.dot(both[...], stack_h, preferred_element_type=F32)
    rest = jnp.dot(both[0:m, :], stack_l, preferred_element_type=F32)
    partial[0:m, start:end] = top[0:m] + (top[m : 2 * m] + rest)


def shifted_sum(partial, start, rows, group):
    total = jnp.zeros((rows, CHUNK), F32)
    for a in range(-(-KS // group)):
        window = partial[a * rows : (a + 1) * rows, start : start + CHUNK + 2 * PAD]
        shift = PAD + group * a - HALF
        total = total + window[:, shift : shift + CHUNK]
    return total


def store_split(high, low, row, column, values):
    h, l = split(values)
    high[row : row + values.shape[0], column : column + values.shape[1]] = h
    low[row : row + values.shape[0], column : column + values.shape[1]] = l


def store_both(both, values):
    h, l = split(values)
    m = values.shape[0]
    both[0:m, :] = h
    both[m : 2 * m, :] = l


def flips(nv):
    return [1 << bit for bit in range(nv.bit_length() - 1)]


def greet(nv, nr):
    v, r = lax.axis_index("visit"), lax.axis_index("row")
    barrier = pltpu.get_barrier_semaphore()

    def hello(a, b):
        pl.semaphore_signal(barrier, inc=1, device_id=(a, b), device_id_type=MESH)

    for flip in flips(nv):
        hello(across(v, flip), r)

    @pl.when(r > 0)
    def _():
        hello(v, r - 1)

    @pl.when(r < nr - 1)
    def _():
        hello(v, r + 1)


def greeted(nv, nr):
    r = lax.axis_index("row")
    above, below = (r > 0).astype(jnp.int32), (r < nr - 1).astype(jnp.int32)
    pl.semaphore_wait(pltpu.get_barrier_semaphore(), len(flips(nv)) + above + below)


def across(v, flip):
    return v + flip - 2 * flip * ((v // flip) % 2)


def remote(src, dst, send, recv, device):
    return pltpu.make_async_remote_copy(
        src_ref=src, dst_ref=dst, send_sem=send, recv_sem=recv, device_id=device, device_id_type=MESH
    )


BEGIN, SHARES_AT = 3.3, 2.0
NEAR_PER, NEAR_DELAY, HOP_PER, HOP_DELAY = 6e-6, 0.9, 7.2e-5, 2.3
COSTS = {"number_step": 0.08, "share_forward": 0.08, "subtract": 0.15, "finish": 0.6, "advance": 0.75, "match": 2e-4}


def whole_kernel(
    nv, nr, science_in, basis_in, coeffs_in, row_starts_in, row_taps_in, offsets, col_starts_in, col_taps_in,
    weights, masks_in, decor_in,
    cleaned, template,
    science, basis, coeffs, row_starts, row_taps, col_starts, col_taps, masks, decor, load_sems,
    shares, share_landed, share_sums, numbers, number_landed, number_sums, gathered, warped,
    near_top, near_bottom, packs, pairs_top, pairs_bottom, edges_out, edges_in,
    square, bands, flat, both, second_flat, second_both,
    high, low, second_high, second_low, partial, shifted, mover,
    share_sems, number_sems, halo_sems, late_sems,
):
    v, r = lax.axis_index("visit"), lax.axis_index("row")
    rows, columns = science.shape
    width = columns // nv
    parity = v % 2
    turns = flips(nv)
    devices = [(across(v, flip), r) for flip in turns]
    chunks = packs.shape[1]
    span = columns // chunks
    part = columns // SUM_PARTS
    half = part // 2
    joined = SUM_PARTS // SHARE_PARTS
    padded = padded_width(columns)
    depth, group = high.shape[0], 3
    second_depth, second_group = second_high.shape[0], 4
    middle = rows + 2 * TAPS

    greet(nv, nr)
    loads = [
        pltpu.make_async_copy(src, dst, load_sems.at[n])
        for n, (src, dst) in enumerate([
            (science_in, science), (col_starts_in, col_starts),
            (masks_in, masks), (coeffs_in, coeffs), (basis_in, basis), (row_starts_in, row_starts),
            (row_taps_in, row_taps), (decor_in, decor), (col_taps_in, col_taps),
        ])
    ]
    for load in loads:
        load.start()
    loads[0].wait()
    quarter = span // 4
    for n in range(chunks):
        for q in range(4):
            at = n * span + q * quarter
            packs[0, n, 2 * q : 2 * q + 2, :] = science[16:18, at : at + quarter]
            packs[1, n, 2 * q : 2 * q + 2, :] = science[rows - 18 : rows - 16, at : at + quarter]
    greeted(nv, nr)
    up, down = [], []
    for n in range(chunks):
        cols = slice(n * span, (n + 1) * span)
        up.append(remote(science.at[0:16, cols], near_bottom.at[:, cols], halo_sems.at[0, n], halo_sems.at[1, n], (v, r - 1)))
        up.append(remote(packs.at[0, n], pairs_bottom.at[n], halo_sems.at[2, n], halo_sems.at[3, n], (v, r - 1)))
        down.append(remote(science.at[rows - 16 : rows, cols], near_top.at[:, cols], halo_sems.at[4, n], halo_sems.at[5, n], (v, r + 1)))
        down.append(remote(packs.at[1, n], pairs_top.at[n], halo_sems.at[6, n], halo_sems.at[7, n], (v, r + 1)))

    @pl.when(r > 0)
    def _():
        for copy in up:
            copy.start()

    @pl.when(r < nr - 1)
    def _():
        for copy in down:
            copy.start()

    for load in loads[1:]:
        load.wait()
    dither = offsets[0]

    def place_of(c):
        return c // joined, slice((c % joined) * half, (c % joined + 1) * half)

    def share_copy(step, w):
        src = shares.at[1 - parity, w] if step == 0 else share_sums.at[step - 1, w]
        return remote(src, share_landed.at[step, w], share_sems.at[0, step, w], share_sems.at[1, step, w], devices[step])

    for w in range(SHARE_PARTS):
        for c in range(w * joined, (w + 1) * joined):
            for h in range(2):
                at = c * part + h * half
                cols = slice(at, at + half)
                start = col_starts[:, cols] + (lax.broadcasted_iota(jnp.int32, (1, half), 1) + (at - dither))
                covered = jnp.where((start >= 0) & (start <= columns - TAPS), weights[0], 0.0)
                shares[h, w, :, place_of(c)[1]] = masks[:, cols].astype(F32) * covered
        share_copy(0, w).start()

    @pl.when(r == 0)
    def _():
        near_top[...] = jnp.zeros_like(near_top)
        pairs_top[...] = jnp.zeros_like(pairs_top)
        edges_in[0] = jnp.zeros_like(edges_in[0])

    @pl.when(r == nr - 1)
    def _():
        near_bottom[...] = jnp.zeros_like(near_bottom)
        pairs_bottom[...] = jnp.zeros_like(pairs_bottom)
        edges_in[1] = jnp.zeros_like(edges_in[1])

    kernel = coeffs[0] * basis[0]
    for b in range(1, basis.shape[0]):
        kernel = kernel + coeffs[b] * basis[b]
    kernel_t = kernel_transposed(kernel, square)
    m = lax.broadcasted_iota(jnp.int32, (middle, rows), 0) - TAPS
    i = lax.broadcasted_iota(jnp.int32, (middle, rows), 1)
    tap = m - i - row_starts[...]
    inside = (m + r * rows >= 0) & (m + r * rows < nr * rows)
    mix = jnp.zeros((middle, rows), F32)
    for t in range(TAPS):
        mix = mix + jnp.where((tap == t) & inside, row_taps[t : t + 1, :], 0.0)
    for c in range(KS):
        bands[:, c * 128 : (c + 1) * 128] = toeplitz(kernel_t, c, middle, 6)
    folded = lax.dot_general(
        mix, bands[...], (((0,), (0,)), ((), ())), precision=lax.Precision.HIGHEST, preferred_element_type=F32
    )
    flat[...] = jnp.zeros_like(flat)
    for c in range(KS):
        a, b = c // group, c % group
        flat[a * rows : (a + 1) * rows, b * depth : (b + 1) * depth] = folded[:, c * 128 : c * 128 + depth]
    store_both(both, flat[...])

    summed = set()

    def share_step(step, w):
        share_copy(step, w).wait()
        before = shares[parity, w] if step == 0 else share_sums[step - 1, w]
        share_sums[step, w] = before + share_landed[step, w]
        summed.add((step, w))
        if step + 1 < len(turns):
            share_copy(step + 1, w).start()

    for w in range(SHARE_PARTS):
        share_step(0, w)

    kernel_t = kernel_transposed(decor[:, 0, :], square)
    second_flat[...] = jnp.zeros_like(second_flat)
    for c in range(KS):
        band = toeplitz(kernel_t, c, rows, 6)
        a, b = c // second_group, c % second_group
        here = slice(a * rows, (a + 1) * rows)
        second_flat[here, b * second_depth : (b + 1) * second_depth] = band[:, 0:second_depth]
    store_both(second_both, second_flat[...])

    for frame in (high, low, second_high, second_low):
        frame[...] = jnp.zeros_like(frame)
    shifted[...] = jnp.zeros_like(shifted)

    tiles = jnp.full((rows, CHUNK + 384), dither // 128, jnp.int32)
    place = lax.broadcasted_iota(jnp.int32, (256, 128), 0) - lax.broadcasted_iota(jnp.int32, (256, 128), 1)
    mover[...] = jnp.where(place == 128 - dither % 128, 1.0, 0.0).astype(BF16)

    def warp(u):
        start = u * CHUNK
        count = CHUNK // 128 + 2
        window = shifted[:, start + 384 : start + 768 + CHUNK]
        for t in range(1, 4):
            at = start + 384 - 128 * t
            window = jnp.where(tiles == t, shifted[:, at : at + CHUNK + 384], window)
        h, l = split(window)
        stack_h = jnp.concatenate([h[:, 128 * j : 128 * j + 256] for j in range(count)], axis=0)
        stack_l = jnp.concatenate([l[:, 128 * j : 128 * j + 256] for j in range(count)], axis=0)
        moved = jnp.dot(stack_h, mover[...], preferred_element_type=F32)
        moved = moved + jnp.dot(stack_l, mover[...], preferred_element_type=F32)
        window = jnp.concatenate([moved[j * rows : (j + 1) * rows] for j in range(count)], axis=1)
        cols = slice(start, start + CHUNK)
        early = col_starts[:, cols] == -3
        taps = [col_taps[t : t + 1, cols] for t in range(TAPS)]
        total = jnp.zeros((rows, CHUNK), F32)
        for lag in range(TAPS + 1):
            now = taps[lag] if lag < TAPS else jnp.zeros_like(taps[0])
            before = taps[lag - 1] if lag > 0 else jnp.zeros_like(taps[0])
            at = 128 + lag - 3
            total = total + jnp.where(early, now, before) * window[:, at : at + CHUNK]
        warped[:, cols] = total
        for n in range(CHUNK // half):
            c, h = (start // half + n) // 2, (start // half + n) % 2
            w, at = place_of(c)
            numbers[c, h] = shares[h, w, :, at] * total[:, n * half : (n + 1) * half]

    last = len(turns)

    def number_copy(step, c):
        sems = number_sems.at[0, step, c], number_sems.at[1, step, c]
        if step == last:
            return remote(gathered.at[c, parity], gathered.at[c, parity], *sems, devices[0])
        src = numbers.at[c, 1 - parity] if step == 0 else number_sums.at[step - 1, c]
        return remote(src, number_landed.at[step, c], *sems, devices[step])

    def late_copies(c):
        return (
            remote(edges_out.at[0, c], edges_in.at[1, c], late_sems.at[0, c], late_sems.at[1, c], (v, r - 1)),
            remote(edges_out.at[1, c], edges_in.at[0, c], late_sems.at[2, c], late_sems.at[3, c], (v, r + 1)),
        )

    queue, clock, free = [], BEGIN, {}
    done = {"pieces": 0, "sums": 0, "warps": 0, "parts": 0, "second": 0, "outs": 0}
    starts = [n * CHUNK for n in range(-(-padded // CHUNK))]
    ends = [min(at + CHUNK, padded) for at in starts]
    order = iter(range(1 << 20))

    def later(link, elements, action):
        per, delay = (NEAR_PER, NEAR_DELAY) if link == 0 else (HOP_PER, HOP_DELAY)
        free[link] = max(clock, free.get(link, 0.0)) + per * elements
        heapq.heappush(queue, (free[link] + delay, next(order), action))

    def number_step(step, c):
        number_copy(step, c).wait()
        before = numbers[c, parity] if step == 0 else number_sums[step - 1, c]
        total = before + number_landed[step, c]
        if step + 1 < last:
            number_sums[step, c] = total
            number_copy(step + 1, c).start()
            later(step + 1, rows * half, functools.partial(number_step, step + 1, c))
            return
        w, at = place_of(c)
        assert (last - 1, w) in summed
        gathered[c, parity] = total / jnp.maximum(share_sums[last - 1, w, :, at], 1.0)
        number_copy(last, c).start()
        later(0, rows * half, functools.partial(subtract, c))

    def subtract(c):
        number_copy(last, c).wait()
        for h in range(2):
            at = c * part + h * half
            cols = slice(at, at + half)
            values = warped[:, cols] - gathered[c, h]
            hi, lo = split(values)
            second_high[16 : 16 + rows, PAD + at : PAD + at + half] = hi
            second_low[16 : 16 + rows, PAD + at : PAD + at + half] = lo
            here = slice(h * half, (h + 1) * half)
            edges_out[0, c, :, here] = values[0:8]
            edges_out[1, c, :, here] = values[rows - 8 : rows]
            for q in range(2):
                cut = slice(q * (half // 2), (q + 1) * (half // 2))
                k = 4 * h + 2 * q
                edges_out[0, c, k : k + 2, part : part + half // 2] = values[8:10, cut]
                edges_out[1, c, k : k + 2, part : part + half // 2] = values[rows - 10 : rows - 8, cut]
        to_above, to_below = late_copies(c)

        @pl.when(r > 0)
        def _():
            to_above.start()

        @pl.when(r < nr - 1)
        def _():
            to_below.start()

        later("row", edges_out[0, c].size, functools.partial(finish, c))

    def finish(c):
        to_above, to_below = late_copies(c)

        @pl.when(r > 0)
        def _():
            to_below.wait_recv()

        @pl.when(r < nr - 1)
        def _():
            to_above.wait_recv()

        at = PAD + c * part
        frames = second_high, second_low
        store_split(*frames, 8, at, edges_in[0, c, :, 0:part])
        store_split(*frames, 16 + rows, at, edges_in[1, c, :, 0:part])
        for q in range(4):
            cut = at + q * (half // 2)
            store_split(*frames, 6, cut, edges_in[0, c, 2 * q : 2 * q + 2, part : part + half // 2])
            store_split(*frames, 24 + rows, cut, edges_in[1, c, 2 * q : 2 * q + 2, part : part + half // 2])
        while done["second"] < len(starts) and (c == SUM_PARTS - 1 or ends[done["second"]] + 8 - PAD <= (c + 1) * part):
            n = done["second"]
            piece(second_high, second_low, second_both, partial, starts[n], ends[n], second_group)
            done["second"] += 1
            if n > 0:
                cleaned[:, starts[n - 1] : starts[n]] = shifted_sum(partial, starts[n - 1], rows, second_group)

    def match(n):
        cols = slice(n * span, (n + 1) * span)

        @pl.when(r > 0)
        def _():
            down[2 * n].wait_recv()
            down[2 * n + 1].wait_recv()

        @pl.when(r < nr - 1)
        def _():
            up[2 * n].wait_recv()
            up[2 * n + 1].wait_recv()

        store_split(high, low, 24, PAD + n * span, science[:, cols])
        store_split(high, low, 8, PAD + n * span, near_top[:, cols])
        store_split(high, low, 24 + rows, PAD + n * span, near_bottom[:, cols])
        for q in range(4):
            at = PAD + n * span + q * quarter
            store_split(high, low, 6, at, pairs_top[n, 2 * q : 2 * q + 2, :])
            store_split(high, low, 40 + rows, at, pairs_bottom[n, 2 * q : 2 * q + 2, :])

    def advance(ready):
        n = done["pieces"]
        if n < len(starts) and enough(ready):
            piece(high, low, both, partial, starts[n], ends[n], group)
            done["pieces"] += 1
            return True
        return False

    def enough(ready):
        n = done["pieces"]
        return n >= len(starts) or ready == columns or ends[n] + group - PAD <= ready

    def warps():
        while done["sums"] < columns // CHUNK and done["sums"] + 2 <= done["pieces"]:
            start = done["sums"] * CHUNK
            shifted[:, 640 + start : 640 + start + CHUNK] = shifted_sum(partial, start, rows, group)
            done["sums"] += 1
        while done["warps"] < columns // CHUNK and (
            done["sums"] * CHUNK >= (done["warps"] + 1) * CHUNK + 8 or done["sums"] * CHUNK == columns
        ):
            warp(done["warps"])
            done["warps"] += 1
        while (done["parts"] + 1) * part <= done["warps"] * CHUNK:
            number_copy(0, done["parts"]).start()
            later(0, rows * half, functools.partial(number_step, 0, done["parts"]))
            done["parts"] += 1

    def share_forward(step, w):
        share_step(step, w)
        if step + 1 < last:
            later(step + 1, rows * half * joined, functools.partial(share_forward, step + 1, w))

    for w in range(SHARE_PARTS):
        clock = SHARES_AT
        later(1, rows * half * joined, functools.partial(share_forward, 1, w))
    clock = BEGIN
    landed = [HOP_DELAY + (n + 1) * span * 18 * HOP_PER for n in range(chunks)]
    arrived = 0
    while queue or done["warps"] < columns // CHUNK:
        working = done["warps"] < columns // CHUNK
        ready = clock
        if working and arrived < chunks and not enough(arrived * span):
            ready = max(clock, landed[arrived])
        if queue and (not working or queue[0][0] <= ready):
            at, _, action = heapq.heappop(queue)
            clock = max(clock, at)
            action()
            clock += COSTS[action.func.__name__]
            continue
        clock = ready
        if advance(arrived * span):
            clock += COSTS["advance"]
            warps()
        else:
            match(arrived)
            arrived += 1
            clock += COSTS["match"] * span

    if half <= width:
        for k in range(width // half):
            n = v * (width // half) + k
            template[:, k * half : (k + 1) * half] = gathered[n // 2, n % 2]
    else:
        n = v * width // half
        template[...] = gathered[n // 2, n % 2, :, pl.ds(pl.multiple_of((v * width) % half, width), width)]

    for c in range(SUM_PARTS):
        to_above, to_below = late_copies(c)

        @pl.when(r > 0)
        def _():
            to_above.wait_send()

        @pl.when(r < nr - 1)
        def _():
            to_below.wait_send()

    @pl.when(r > 0)
    def _():
        for copy in up:
            copy.wait_send()

    @pl.when(r < nr - 1)
    def _():
        for copy in down:
            copy.wait_send()


def hand_over(cleaned, template, cleaned_out, template_out, sems):
    first = pltpu.make_async_copy(cleaned, cleaned_out, sems.at[0])
    second = pltpu.make_async_copy(template, template_out, sems.at[1])
    first.start()
    second.start()
    first.wait()
    second.wait()


def shape(*dims):
    return jax.ShapeDtypeStruct(dims, F32)


def in_hbm(array):
    return pltpu.with_memory_space_constraint(array, pltpu.HBM)


def on_device(
    nv, nr, science, basis_kernels, basis_coeffs, row_starts, row_taps, col_offsets,
    col_starts, col_taps, visit_weights, clip_masks, decorrelation,
):
    pixels = science[0]
    rows, columns = pixels.shape
    width = columns // nv
    padded = padded_width(columns)
    depth, group = 80, 3
    tall = -(-KS // group) * rows
    second_depth, second_group = rows + 32, 4
    wide = -(-KS // second_group) * rows
    part, span = columns // SUM_PARTS, columns // HALO_PARTS
    half, share_half, turns = part // 2, columns // SHARE_PARTS // 2, len(flips(nv))
    f32 = lambda *dims: pltpu.VMEM(dims, F32)
    bf16 = lambda *dims: pltpu.VMEM(dims, BF16)
    cleaned, template = pl.pallas_call(
        functools.partial(whole_kernel, nv, nr),
        out_shape=(pltpu.VMEM((rows, columns), F32), pltpu.VMEM((rows, width), F32)),
        in_specs=[HBM] * 5 + [SMEM] + [HBM] * 2 + [SMEM] + [HBM] * 2,
        out_specs=(VMEM, VMEM),
        scratch_shapes=[
            f32(rows, columns), f32(*basis_kernels.shape), pltpu.SMEM(basis_coeffs.shape[1:], F32),
            pltpu.VMEM((1, rows), jnp.int32), f32(TAPS, rows),
            pltpu.VMEM((1, columns), jnp.int32), f32(TAPS, columns),
            pltpu.VMEM((rows, columns), jnp.int32), f32(KS, 1, KS), pltpu.SemaphoreType.DMA((9,)),
            f32(2, SHARE_PARTS, rows, share_half), f32(turns, SHARE_PARTS, rows, share_half),
            f32(turns, SHARE_PARTS, rows, share_half),
            f32(SUM_PARTS, 2, rows, half), f32(turns, SUM_PARTS, rows, half), f32(turns - 1, SUM_PARTS, rows, half),
            f32(SUM_PARTS, 2, rows, half), f32(rows, columns),
            f32(16, columns), f32(16, columns), f32(2, HALO_PARTS, 8, span // 4),
            f32(HALO_PARTS, 8, span // 4), f32(HALO_PARTS, 8, span // 4),
            f32(2, SUM_PARTS, 8, part + half // 2), f32(2, SUM_PARTS, 8, part + half // 2),
            f32(128, 128), f32(rows + 2 * TAPS, KS * 128),
            f32(tall, group * depth), bf16(2 * tall, group * depth),
            f32(wide, second_group * second_depth), bf16(2 * wide, second_group * second_depth),
            bf16(depth, padded + 128), bf16(depth, padded + 128),
            bf16(second_depth, padded + 128), bf16(second_depth, padded + 128),
            f32(tall, padded), f32(rows, columns + 1024), bf16(256, 128),
            pltpu.SemaphoreType.DMA((2, turns, SHARE_PARTS)),
            pltpu.SemaphoreType.DMA((2, turns + 1, SUM_PARTS)),
            pltpu.SemaphoreType.DMA((8, HALO_PARTS)),
            pltpu.SemaphoreType.DMA((4, SUM_PARTS)),
        ],
        compiler_params=pltpu.CompilerParams(
            collective_id=0, has_side_effects=True, vmem_limit_bytes=28 * 1024 * 1024
        ),
        name="whole",
    )(
        *map(in_hbm, (pixels, basis_kernels, basis_coeffs[0], row_starts, row_taps[0])), col_offsets,
        *map(in_hbm, (col_starts, col_taps[0])), visit_weights,
        *map(in_hbm, (clip_masks[0], jnp.transpose(decorrelation, (1, 0, 2)))),
    )
    cleaned, template = pl.pallas_call(
        hand_over,
        out_shape=(shape(rows, columns), shape(rows, width)),
        in_specs=[VMEM, VMEM],
        out_specs=(HBM, HBM),
        scratch_shapes=[pltpu.SemaphoreType.DMA((2,))],
        compiler_params=pltpu.CompilerParams(vmem_limit_bytes=8 * 1024 * 1024),
        name="hand_over",
    )(cleaned, template)
    return (cleaned[None], template)


def solution(mesh):
    nv, nr = mesh.shape["visit"], mesh.shape["row"]
    return jax.shard_map(
        functools.partial(on_device, nv, nr),
        mesh=mesh,
        in_specs=(
            P("visit", "row", None),
            P(),
            P("visit", None),
            P("visit", "row"),
            P("visit", None, "row"),
            P("visit"),
            P("visit", None),
            P("visit", None, None),
            P("visit"),
            P("visit", "row", None),
            P("visit", None, None),
        ),
        out_specs=(P("visit", "row", None), P("row", "visit")),
        check_vma=False,
    )
```

```python
import functools
import heapq

import jax
import jax.numpy as jnp
from jax import lax
from jax.experimental import pallas as pl
from jax.experimental.pallas import tpu as pltpu
from jax.sharding import PartitionSpec as P

KS = 21
HALF = KS // 2
TAPS = 8
PAD = 128
CHUNK = 512
HALO_PARTS = 8
SUM_PARTS = 8
SHARE_PARTS = 4
F32 = jnp.float32
BF16 = jnp.bfloat16
MESH = pl.DeviceIdType.MESH
VMEM = pl.BlockSpec(memory_space=pltpu.VMEM)
HBM = pl.BlockSpec(memory_space=pltpu.HBM)
SMEM = pl.BlockSpec(memory_space=pltpu.SMEM)


def padded_width(columns):
    return -(-(columns + 2 * PAD) // PAD) * PAD


def split(x):
    high = x.astype(BF16)
    low = (x - high.astype(F32)).astype(BF16)
    return high, low


def toeplitz(kernel_t, c, rows, lead):
    line = jnp.broadcast_to(kernel_t[c : c + 1, :], (rows, 128))
    return pltpu.roll(line, lead, 1, stride=1, stride_axis=0)


def kernel_transposed(kernel, square):
    square[...] = jnp.zeros_like(square)
    square[0:KS, 0:KS] = kernel
    return jnp.transpose(square[...])


def piece(high, low, both, partial, start, end, group):
    m, wide = both.shape[0] // 2, end - start
    window_h = high[:, start : end + 128]
    window_l = low[:, start : end + 128]
    stack_h = jnp.concatenate([window_h[:, b : b + wide] for b in range(group)], axis=0)
    stack_l = jnp.concatenate([window_l[:, b : b + wide] for b in range(group)], axis=0)
    top = jnp.dot(both[...], stack_h, preferred_element_type=F32)
    rest = jnp.dot(both[0:m, :], stack_l, preferred_element_type=F32)
    partial[0:m, start:end] = top[0:m] + (top[m : 2 * m] + rest)


def shifted_sum(partial, start, end, rows, group):
    total = jnp.zeros((rows, end - start), F32)
    for a in range(-(-KS // group)):
        window = partial[a * rows : (a + 1) * rows, start : end + 2 * PAD]
        shift = PAD + group * a - HALF
        total = total + window[:, shift : shift + end - start]
    return total


def store_split(high, low, row, column, values):
    h, l = split(values)
    high[row : row + values.shape[0], column : column + values.shape[1]] = h
    low[row : row + values.shape[0], column : column + values.shape[1]] = l


def store_both(both, values):
    h, l = split(values)
    m = values.shape[0]
    both[0:m, :] = h
    both[m : 2 * m, :] = l


def flips(nv):
    return [1 << bit for bit in range(nv.bit_length() - 1)]


def greet(nv, nr):
    v, r = lax.axis_index("visit"), lax.axis_index("row")
    barrier = pltpu.get_barrier_semaphore()

    def hello(a, b):
        pl.semaphore_signal(barrier, inc=1, device_id=(a, b), device_id_type=MESH)

    for flip in flips(nv):
        hello(across(v, flip), r)

    @pl.when(r > 0)
    def _():
        hello(v, r - 1)
        hello(across(v, 1), r - 1)

    @pl.when(r < nr - 1)
    def _():
        hello(v, r + 1)
        hello(across(v, 1), r + 1)


def greeted(nv, nr):
    r = lax.axis_index("row")
    above, below = (r > 0).astype(jnp.int32), (r < nr - 1).astype(jnp.int32)
    pl.semaphore_wait(pltpu.get_barrier_semaphore(), len(flips(nv)) + 2 * above + 2 * below)


def across(v, flip):
    return v + flip - 2 * flip * ((v // flip) % 2)


def remote(src, dst, send, recv, device):
    return pltpu.make_async_remote_copy(
        src_ref=src, dst_ref=dst, send_sem=send, recv_sem=recv, device_id=device, device_id_type=MESH
    )


BEGIN, SHARES_AT = 3.3, 2.0
NEAR_PER, NEAR_DELAY, HOP_PER, HOP_DELAY = 6e-6, 0.9, 7.2e-5, 2.3
COSTS = {"number_step": 0.08, "share_forward": 0.08, "subtract": 0.15, "finish": 0.6, "advance": 0.75, "match": 2e-4}


def whole_kernel(
    nv, nr, science_in, basis_in, coeffs_in, row_starts_in, row_taps_in, offsets, col_starts_in, col_taps_in,
    weights, masks_in, decor_in,
    cleaned, template,
    science, basis, coeffs, row_starts, row_taps, col_starts, col_taps, masks, decor, load_sems,
    shares, share_landed, share_sums, numbers, number_landed, number_sums, gathered, warped,
    near_top, near_bottom, packs, pairs_top, pairs_bottom, edges_out, edges_in, borders,
    square, bands, flat, both, second_flat, second_both,
    high, low, second_high, second_low, partial, shifted, mover,
    share_sems, number_sems, halo_sems, late_sems, border_sems,
):
    v, r = lax.axis_index("visit"), lax.axis_index("row")
    rows, columns = science.shape
    width = columns // nv
    parity = v % 2
    turns = flips(nv)
    devices = [(across(v, 1), r)]
    for n in range(1, len(turns)):
        ahead, back = across(v, turns[n]), across(v, turns[len(turns) - n])
        devices.append((ahead + parity * (back - ahead), r))
    chunks = packs.shape[1]
    span = columns // chunks
    part = columns // SUM_PARTS
    half = part // 2
    joined = SUM_PARTS // SHARE_PARTS
    padded = padded_width(columns)
    depth, group = high.shape[0], 3
    second_depth, second_group = second_high.shape[0], 4
    middle = rows + 2 * TAPS

    greet(nv, nr)
    loads = [
        pltpu.make_async_copy(src, dst, load_sems.at[n])
        for n, (src, dst) in enumerate([
            (science_in, science), (col_starts_in, col_starts),
            (masks_in, masks), (coeffs_in, coeffs), (basis_in, basis), (row_starts_in, row_starts),
            (row_taps_in, row_taps), (decor_in, decor), (col_taps_in, col_taps),
        ])
    ]
    for load in loads:
        load.start()
    loads[0].wait()
    quarter = span // 4
    for n in range(chunks):
        for q in range(4):
            at = n * span + q * quarter
            packs[0, n, 2 * q : 2 * q + 2, :] = science[16:18, at : at + quarter]
            packs[1, n, 2 * q : 2 * q + 2, :] = science[rows - 18 : rows - 16, at : at + quarter]
    greeted(nv, nr)
    up, down = [], []
    for n in range(chunks):
        cols = slice(n * span, (n + 1) * span)
        up.append(remote(science.at[0:16, cols], near_bottom.at[:, cols], halo_sems.at[0, n], halo_sems.at[1, n], (v, r - 1)))
        up.append(remote(packs.at[0, n], pairs_bottom.at[n], halo_sems.at[2, n], halo_sems.at[3, n], (v, r - 1)))
        down.append(remote(science.at[rows - 16 : rows, cols], near_top.at[:, cols], halo_sems.at[4, n], halo_sems.at[5, n], (v, r + 1)))
        down.append(remote(packs.at[1, n], pairs_top.at[n], halo_sems.at[6, n], halo_sems.at[7, n], (v, r + 1)))

    @pl.when(r > 0)
    def _():
        for copy in up:
            copy.start()

    @pl.when(r < nr - 1)
    def _():
        for copy in down:
            copy.start()

    for load in loads[1:]:
        load.wait()
    dither = offsets[0]

    def place_of(c):
        return c // joined, slice((c % joined) * half, (c % joined + 1) * half)

    def share_copy(step, w):
        src = shares.at[1 - parity, w] if step == 0 else share_sums.at[step - 1, w]
        return remote(src, share_landed.at[step, w], share_sems.at[0, step, w], share_sems.at[1, step, w], devices[step])

    for w in range(SHARE_PARTS):
        for c in range(w * joined, (w + 1) * joined):
            for h in range(2):
                at = c * part + h * half
                cols = slice(at, at + half)
                start = col_starts[:, cols] + (lax.broadcasted_iota(jnp.int32, (1, half), 1) + (at - dither))
                covered = jnp.where((start >= 0) & (start <= columns - TAPS), weights[0], 0.0)
                shares[h, w, :, place_of(c)[1]] = masks[:, cols].astype(F32) * covered
        share_copy(0, w).start()

    @pl.when(r == 0)
    def _():
        near_top[...] = jnp.zeros_like(near_top)
        pairs_top[...] = jnp.zeros_like(pairs_top)
        edges_in[0] = jnp.zeros_like(edges_in[0])
        borders[0] = jnp.zeros_like(borders[0])

    @pl.when(r == nr - 1)
    def _():
        near_bottom[...] = jnp.zeros_like(near_bottom)
        pairs_bottom[...] = jnp.zeros_like(pairs_bottom)
        edges_in[1] = jnp.zeros_like(edges_in[1])
        borders[1] = jnp.zeros_like(borders[1])

    kernel = coeffs[0] * basis[0]
    for b in range(1, basis.shape[0]):
        kernel = kernel + coeffs[b] * basis[b]
    kernel_t = kernel_transposed(kernel, square)
    m = lax.broadcasted_iota(jnp.int32, (middle, rows), 0) - TAPS
    i = lax.broadcasted_iota(jnp.int32, (middle, rows), 1)
    tap = m - i - row_starts[...]
    inside = (m + r * rows >= 0) & (m + r * rows < nr * rows)
    mix = jnp.zeros((middle, rows), F32)
    for t in range(TAPS):
        mix = mix + jnp.where((tap == t) & inside, row_taps[t : t + 1, :], 0.0)
    for c in range(KS):
        bands[:, c * 128 : (c + 1) * 128] = toeplitz(kernel_t, c, middle, 6)
    folded = lax.dot_general(
        mix, bands[...], (((0,), (0,)), ((), ())), precision=lax.Precision.HIGHEST, preferred_element_type=F32
    )
    flat[...] = jnp.zeros_like(flat)
    for c in range(KS):
        a, b = c // group, c % group
        flat[a * rows : (a + 1) * rows, b * depth : (b + 1) * depth] = folded[:, c * 128 : c * 128 + depth]
    store_both(both, flat[...])

    summed, subtracted = set(), set()

    def share_step(step, w):
        share_copy(step, w).wait()
        before = shares[parity, w] if step == 0 else share_sums[step - 1, w]
        share_sums[step, w] = before + share_landed[step, w]
        summed.add((step, w))
        if step + 1 < len(turns):
            share_copy(step + 1, w).start()

    for w in range(SHARE_PARTS):
        share_step(0, w)

    kernel_t = kernel_transposed(decor[:, 0, :], square)
    second_flat[...] = jnp.zeros_like(second_flat)
    for c in range(KS):
        band = toeplitz(kernel_t, c, rows, 6)
        a, b = c // second_group, c % second_group
        here = slice(a * rows, (a + 1) * rows)
        second_flat[here, b * second_depth : (b + 1) * second_depth] = band[:, 0:second_depth]
    store_both(second_both, second_flat[...])

    for frame in (high, low, second_high, second_low):
        frame[...] = jnp.zeros_like(frame)
    shifted[...] = jnp.zeros_like(shifted)

    tiles = jnp.full((rows, CHUNK + 384), dither // 128, jnp.int32)
    place = lax.broadcasted_iota(jnp.int32, (256, 128), 0) - lax.broadcasted_iota(jnp.int32, (256, 128), 1)
    mover[...] = jnp.where(place == 128 - dither % 128, 1.0, 0.0).astype(BF16)

    def warp(u):
        start = u * CHUNK
        count = CHUNK // 128 + 2
        window = shifted[:, start + 384 : start + 768 + CHUNK]
        for t in range(1, 4):
            at = start + 384 - 128 * t
            window = jnp.where(tiles == t, shifted[:, at : at + CHUNK + 384], window)
        h, l = split(window)
        stack_h = jnp.concatenate([h[:, 128 * j : 128 * j + 256] for j in range(count)], axis=0)
        stack_l = jnp.concatenate([l[:, 128 * j : 128 * j + 256] for j in range(count)], axis=0)
        moved = jnp.dot(stack_h, mover[...], preferred_element_type=F32)
        moved = moved + jnp.dot(stack_l, mover[...], preferred_element_type=F32)
        window = jnp.concatenate([moved[j * rows : (j + 1) * rows] for j in range(count)], axis=1)
        cols = slice(start, start + CHUNK)
        early = col_starts[:, cols] == -3
        taps = [col_taps[t : t + 1, cols] for t in range(TAPS)]
        total = jnp.zeros((rows, CHUNK), F32)
        for lag in range(TAPS + 1):
            now = taps[lag] if lag < TAPS else jnp.zeros_like(taps[0])
            before = taps[lag - 1] if lag > 0 else jnp.zeros_like(taps[0])
            at = 128 + lag - 3
            total = total + jnp.where(early, now, before) * window[:, at : at + CHUNK]
        warped[:, cols] = total
        for n in range(CHUNK // half):
            c, h = (start // half + n) // 2, (start // half + n) % 2
            w, at = place_of(c)
            numbers[c, h] = shares[h, w, :, at] * total[:, n * half : (n + 1) * half]

    last = len(turns)

    def number_copy(step, c):
        sems = number_sems.at[0, step, c], number_sems.at[1, step, c]
        if step == last:
            return remote(gathered.at[c, parity], gathered.at[c, parity], *sems, devices[0])
        src = numbers.at[c, 1 - parity] if step == 0 else number_sums.at[step - 1, c]
        return remote(src, number_landed.at[step, c], *sems, devices[step])

    def late_copies(c):
        return (
            remote(edges_out.at[0, c], edges_in.at[1, c], late_sems.at[0, c], late_sems.at[1, c], (v, r - 1)),
            remote(edges_out.at[1, c], edges_in.at[0, c], late_sems.at[2, c], late_sems.at[3, c], (v, r + 1)),
        )

    def border_copies(c, up):
        side, row, src = (1, r - 1, slice(0, 16)) if up else (0, r + 1, slice(rows - 16, rows))
        return [
            remote(
                gathered.at[c, parity, src], borders.at[side, c, parity],
                border_sems.at[0, side, k, c], border_sems.at[1, side, k, c], (column, row),
            )
            for k, column in enumerate((v, across(v, 1)))
        ]

    def outward(c):
        to_above, to_below = late_copies(c)
        for h in range(2):
            at = c * part + h * half
            here = slice(h * half, (h + 1) * half)
            edges_out[0, c, :, here] = warped[0:8, at : at + half]
            edges_out[1, c, :, here] = warped[rows - 8 : rows, at : at + half]
            for q in range(2):
                cut = slice(at + q * (half // 2), at + (q + 1) * (half // 2))
                k = 4 * h + 2 * q
                edges_out[0, c, k : k + 2, part : part + half // 2] = warped[8:10, cut]
                edges_out[1, c, k : k + 2, part : part + half // 2] = warped[rows - 10 : rows - 8, cut]

        @pl.when(r > 0)
        def _():
            to_above.start()

        @pl.when(r < nr - 1)
        def _():
            to_below.start()

    queue, clock, free = [], BEGIN, {}
    done = {"pieces": 0, "sums": 0, "warps": 0, "parts": 0, "second": 0, "outs": 0}
    starts = [n * CHUNK for n in range(-(-padded // CHUNK))]
    ends = [min(at + CHUNK, padded) for at in starts]
    bounds = [0] + [at + PAD for at in starts[1 : columns // CHUNK]] + [columns]
    order = iter(range(1 << 20))

    def later(link, elements, action):
        per, delay = (NEAR_PER, NEAR_DELAY) if link == 0 else (HOP_PER, HOP_DELAY)
        free[link] = max(clock, free.get(link, 0.0)) + per * elements
        heapq.heappush(queue, (free[link] + delay, next(order), action))

    def number_step(step, c):
        number_copy(step, c).wait()
        before = numbers[c, parity] if step == 0 else number_sums[step - 1, c]
        total = before + number_landed[step, c]
        if step + 1 < last:
            number_sums[step, c] = total
            number_copy(step + 1, c).start()
            later(step + 1, rows * half, functools.partial(number_step, step + 1, c))
            return
        w, at = place_of(c)
        assert (last - 1, w) in summed
        gathered[c, parity] = total / jnp.maximum(share_sums[last - 1, w, :, at], 1.0)
        number_copy(last, c).start()

        @pl.when(r > 0)
        def _():
            for copy in border_copies(c, True):
                copy.start()

        @pl.when(r < nr - 1)
        def _():
            for copy in border_copies(c, False):
                copy.start()

        later(0, rows * half, functools.partial(subtract, c))
        later("row", 64 * half, functools.partial(finish, c))

    def subtract(c):
        number_copy(last, c).wait()
        for h in range(2):
            at = c * part + h * half
            cols = slice(at, at + half)
            values = warped[:, cols] - gathered[c, h]
            hi, lo = split(values)
            second_high[16 : 16 + rows, PAD + at : PAD + at + half] = hi
            second_low[16 : 16 + rows, PAD + at : PAD + at + half] = lo
        subtracted.add(c)

    def finish(c):
        assert c in subtracted
        to_above, to_below = late_copies(c)

        @pl.when(r > 0)
        def _():
            to_below.wait_recv()
            for copy in border_copies(c, False):
                copy.wait_recv()

        @pl.when(r < nr - 1)
        def _():
            to_above.wait_recv()
            for copy in border_copies(c, True):
                copy.wait_recv()

        frames = second_high, second_low
        for h in range(2):
            here = slice(h * half, (h + 1) * half)
            at = PAD + c * part + h * half
            store_split(*frames, 8, at, edges_in[0, c, :, here] - borders[0, c, h, 8:16])
            store_split(*frames, 16 + rows, at, edges_in[1, c, :, here] - borders[1, c, h, 0:8])
            for q in range(2):
                cut = slice(q * (half // 2), (q + 1) * (half // 2))
                k, wide = 4 * h + 2 * q, slice(part, part + half // 2)
                store_split(*frames, 6, at + q * (half // 2), edges_in[0, c, k : k + 2, wide] - borders[0, c, h, 6:8, cut])
                store_split(*frames, 24 + rows, at + q * (half // 2), edges_in[1, c, k : k + 2, wide] - borders[1, c, h, 8:10, cut])
        while done["second"] < len(starts) and (c == SUM_PARTS - 1 or ends[done["second"]] + 8 - PAD <= (c + 1) * part):
            n = done["second"]
            piece(second_high, second_low, second_both, partial, starts[n], ends[n], second_group)
            done["second"] += 1
            if n > 0:
                cleaned[:, starts[n - 1] : starts[n]] = shifted_sum(partial, starts[n - 1], starts[n], rows, second_group)

    def match(n):
        cols = slice(n * span, (n + 1) * span)

        @pl.when(r > 0)
        def _():
            down[2 * n].wait_recv()
            down[2 * n + 1].wait_recv()

        @pl.when(r < nr - 1)
        def _():
            up[2 * n].wait_recv()
            up[2 * n + 1].wait_recv()

        store_split(high, low, 24, PAD + n * span, science[:, cols])
        store_split(high, low, 8, PAD + n * span, near_top[:, cols])
        store_split(high, low, 24 + rows, PAD + n * span, near_bottom[:, cols])
        for q in range(4):
            at = PAD + n * span + q * quarter
            store_split(high, low, 6, at, pairs_top[n, 2 * q : 2 * q + 2, :])
            store_split(high, low, 40 + rows, at, pairs_bottom[n, 2 * q : 2 * q + 2, :])

    def advance(ready):
        n = done["pieces"]
        if n < len(starts) and enough(ready):
            piece(high, low, both, partial, starts[n], ends[n], group)
            done["pieces"] += 1
            return True
        return False

    def enough(ready):
        n = done["pieces"]
        return n >= len(starts) or ready == columns or ends[n] + group - PAD <= ready

    def warps():
        while done["sums"] < columns // CHUNK and done["sums"] + 2 <= done["pieces"]:
            start, end = bounds[done["sums"] : done["sums"] + 2]
            shifted[:, 640 + start : 640 + end] = shifted_sum(partial, start, end, rows, group)
            done["sums"] += 1
        while done["warps"] < columns // CHUNK and (
            bounds[done["sums"]] >= (done["warps"] + 1) * CHUNK + 8 or bounds[done["sums"]] == columns
        ):
            warp(done["warps"])
            done["warps"] += 1
        while (done["parts"] + 1) * part <= done["warps"] * CHUNK:
            number_copy(0, done["parts"]).start()
            outward(done["parts"])
            later(0, rows * half, functools.partial(number_step, 0, done["parts"]))
            done["parts"] += 1

    def share_forward(step, w):
        share_step(step, w)
        if step + 1 < last:
            later(step + 1, rows * half * joined, functools.partial(share_forward, step + 1, w))

    for w in range(SHARE_PARTS):
        clock = SHARES_AT
        later(1, rows * half * joined, functools.partial(share_forward, 1, w))
    clock = BEGIN
    landed = [HOP_DELAY + (n + 1) * span * 18 * HOP_PER for n in range(chunks)]
    arrived = 0
    while queue or done["warps"] < columns // CHUNK:
        working = done["warps"] < columns // CHUNK
        ready = clock
        if working and arrived < chunks and not enough(arrived * span):
            ready = max(clock, landed[arrived])
        if queue and (not working or queue[0][0] <= ready):
            at, _, action = heapq.heappop(queue)
            clock = max(clock, at)
            action()
            clock += COSTS[action.func.__name__]
            continue
        clock = ready
        if advance(arrived * span):
            clock += COSTS["advance"]
            warps()
        else:
            match(arrived)
            arrived += 1
            clock += COSTS["match"] * span

    if half <= width:
        for k in range(width // half):
            n = v * (width // half) + k
            template[:, k * half : (k + 1) * half] = gathered[n // 2, n % 2]
    else:
        n = v * width // half
        template[...] = gathered[n // 2, n % 2, :, pl.ds(pl.multiple_of((v * width) % half, width), width)]

    for c in range(SUM_PARTS):
        to_above, to_below = late_copies(c)

        @pl.when(r > 0)
        def _():
            for copy in [to_above] + border_copies(c, True):
                copy.wait_send()

        @pl.when(r < nr - 1)
        def _():
            for copy in [to_below] + border_copies(c, False):
                copy.wait_send()

    @pl.when(r > 0)
    def _():
        for copy in up:
            copy.wait_send()

    @pl.when(r < nr - 1)
    def _():
        for copy in down:
            copy.wait_send()


def hand_over(cleaned, template, cleaned_out, template_out, sems):
    first = pltpu.make_async_copy(cleaned, cleaned_out, sems.at[0])
    second = pltpu.make_async_copy(template, template_out, sems.at[1])
    first.start()
    second.start()
    first.wait()
    second.wait()


def shape(*dims):
    return jax.ShapeDtypeStruct(dims, F32)


def in_hbm(array):
    return pltpu.with_memory_space_constraint(array, pltpu.HBM)


def on_device(
    nv, nr, science, basis_kernels, basis_coeffs, row_starts, row_taps, col_offsets,
    col_starts, col_taps, visit_weights, clip_masks, decorrelation,
):
    pixels = science[0]
    rows, columns = pixels.shape
    width = columns // nv
    padded = padded_width(columns)
    depth, group = 80, 3
    tall = -(-KS // group) * rows
    second_depth, second_group = rows + 32, 4
    wide = -(-KS // second_group) * rows
    part, span = columns // SUM_PARTS, columns // HALO_PARTS
    half, share_half, turns = part // 2, columns // SHARE_PARTS // 2, len(flips(nv))
    f32 = lambda *dims: pltpu.VMEM(dims, F32)
    bf16 = lambda *dims: pltpu.VMEM(dims, BF16)
    cleaned, template = pl.pallas_call(
        functools.partial(whole_kernel, nv, nr),
        out_shape=(pltpu.VMEM((rows, columns), F32), pltpu.VMEM((rows, width), F32)),
        in_specs=[HBM] * 5 + [SMEM] + [HBM] * 2 + [SMEM] + [HBM] * 2,
        out_specs=(VMEM, VMEM),
        scratch_shapes=[
            f32(rows, columns), f32(*basis_kernels.shape), pltpu.SMEM(basis_coeffs.shape[1:], F32),
            pltpu.VMEM((1, rows), jnp.int32), f32(TAPS, rows),
            pltpu.VMEM((1, columns), jnp.int32), f32(TAPS, columns),
            pltpu.VMEM((rows, columns), jnp.int32), f32(KS, 1, KS), pltpu.SemaphoreType.DMA((9,)),
            f32(2, SHARE_PARTS, rows, share_half), f32(turns, SHARE_PARTS, rows, share_half),
            f32(turns, SHARE_PARTS, rows, share_half),
            f32(SUM_PARTS, 2, rows, half), f32(turns, SUM_PARTS, rows, half), f32(turns - 1, SUM_PARTS, rows, half),
            f32(SUM_PARTS, 2, rows, half), f32(rows, columns),
            f32(16, columns), f32(16, columns), f32(2, HALO_PARTS, 8, span // 4),
            f32(HALO_PARTS, 8, span // 4), f32(HALO_PARTS, 8, span // 4),
            f32(2, SUM_PARTS, 8, part + half // 2), f32(2, SUM_PARTS, 8, part + half // 2),
            f32(2, SUM_PARTS, 2, 16, half),
            f32(128, 128), f32(rows + 2 * TAPS, KS * 128),
            f32(tall, group * depth), bf16(2 * tall, group * depth),
            f32(wide, second_group * second_depth), bf16(2 * wide, second_group * second_depth),
            bf16(depth, padded + 128), bf16(depth, padded + 128),
            bf16(second_depth, padded + 128), bf16(second_depth, padded + 128),
            f32(tall, padded), f32(rows, columns + 1024), bf16(256, 128),
            pltpu.SemaphoreType.DMA((2, turns, SHARE_PARTS)),
            pltpu.SemaphoreType.DMA((2, turns + 1, SUM_PARTS)),
            pltpu.SemaphoreType.DMA((8, HALO_PARTS)),
            pltpu.SemaphoreType.DMA((4, SUM_PARTS)),
            pltpu.SemaphoreType.DMA((2, 2, 2, SUM_PARTS)),
        ],
        compiler_params=pltpu.CompilerParams(
            collective_id=0, has_side_effects=True, vmem_limit_bytes=28 * 1024 * 1024
        ),
        name="whole",
    )(
        *map(in_hbm, (pixels, basis_kernels, basis_coeffs[0], row_starts, row_taps[0])), col_offsets,
        *map(in_hbm, (col_starts, col_taps[0])), visit_weights,
        *map(in_hbm, (clip_masks[0], jnp.transpose(decorrelation, (1, 0, 2)))),
    )
    cleaned, template = pl.pallas_call(
        hand_over,
        out_shape=(shape(rows, columns), shape(rows, width)),
        in_specs=[VMEM, VMEM],
        out_specs=(HBM, HBM),
        scratch_shapes=[pltpu.SemaphoreType.DMA((2,))],
        compiler_params=pltpu.CompilerParams(vmem_limit_bytes=8 * 1024 * 1024),
        name="hand_over",
    )(cleaned, template)
    return (cleaned[None], template)


def solution(mesh):
    nv, nr = mesh.shape["visit"], mesh.shape["row"]
    return jax.shard_map(
        functools.partial(on_device, nv, nr),
        mesh=mesh,
        in_specs=(
            P("visit", "row", None),
            P(),
            P("visit", None),
            P("visit", "row"),
            P("visit", None, "row"),
            P("visit"),
            P("visit", None),
            P("visit", None, None),
            P("visit"),
            P("visit", "row", None),
            P("visit", None, None),
        ),
        out_specs=(P("visit", "row", None), P("row", "visit")),
        check_vma=False,
    )
```

```python
import functools
import heapq

import jax
import jax.numpy as jnp
from jax import lax
from jax.experimental import pallas as pl
from jax.experimental.pallas import tpu as pltpu
from jax.sharding import PartitionSpec as P

KS = 21
HALF = KS // 2
TAPS = 8
PAD = 128
CHUNK = 512
HALO_PARTS = 8
SUM_PARTS = 8
SHARE_PARTS = 4
BORDER_PARTS = 3
F32 = jnp.float32
BF16 = jnp.bfloat16
MESH = pl.DeviceIdType.MESH
VMEM = pl.BlockSpec(memory_space=pltpu.VMEM)
HBM = pl.BlockSpec(memory_space=pltpu.HBM)
SMEM = pl.BlockSpec(memory_space=pltpu.SMEM)


def padded_width(columns):
    return -(-(columns + 2 * PAD) // PAD) * PAD


def split(x):
    high = x.astype(BF16)
    low = (x - high.astype(F32)).astype(BF16)
    return high, low


def toeplitz(kernel_t, c, rows, lead):
    line = jnp.broadcast_to(kernel_t[c : c + 1, :], (rows, 128))
    return pltpu.roll(line, lead, 1, stride=1, stride_axis=0)


def kernel_transposed(kernel, square):
    square[...] = jnp.zeros_like(square)
    square[0:KS, 0:KS] = kernel
    return jnp.transpose(square[...])


def piece(high, low, both, partial, start, end, group):
    m, wide = both.shape[0] // 2, end - start
    window_h = high[:, start : end + 128]
    window_l = low[:, start : end + 128]
    stack_h = jnp.concatenate([window_h[:, b : b + wide] for b in range(group)], axis=0)
    stack_l = jnp.concatenate([window_l[:, b : b + wide] for b in range(group)], axis=0)
    top = jnp.dot(both[...], stack_h, preferred_element_type=F32)
    rest = jnp.dot(both[0:m, :], stack_l, preferred_element_type=F32)
    partial[0:m, start:end] = top[0:m] + (top[m : 2 * m] + rest)


def shifted_sum(partial, start, end, rows, group):
    total = jnp.zeros((rows, end - start), F32)
    for a in range(-(-KS // group)):
        window = partial[a * rows : (a + 1) * rows, start : end + 2 * PAD]
        shift = PAD + group * a - HALF
        total = total + window[:, shift : shift + end - start]
    return total


def store_split(high, low, row, column, values):
    h, l = split(values)
    high[row : row + values.shape[0], column : column + values.shape[1]] = h
    low[row : row + values.shape[0], column : column + values.shape[1]] = l


def store_both(both, values):
    h, l = split(values)
    m = values.shape[0]
    both[0:m, :] = h
    both[m : 2 * m, :] = l


def flips(nv):
    return [1 << bit for bit in range(nv.bit_length() - 1)]


def greet(nv, nr):
    v, r = lax.axis_index("visit"), lax.axis_index("row")
    barrier = pltpu.get_barrier_semaphore()

    def hello(a, b):
        pl.semaphore_signal(barrier, inc=1, device_id=(a, b), device_id_type=MESH)

    for flip in flips(nv):
        hello(across(v, flip), r)

    @pl.when(r > 0)
    def _():
        hello(v, r - 1)
        hello(across(v, 1), r - 1)

    @pl.when(r < nr - 1)
    def _():
        hello(v, r + 1)
        hello(across(v, 1), r + 1)


def greeted(nv, nr):
    r = lax.axis_index("row")
    above, below = (r > 0).astype(jnp.int32), (r < nr - 1).astype(jnp.int32)
    pl.semaphore_wait(pltpu.get_barrier_semaphore(), len(flips(nv)) + 2 * above + 2 * below)


def across(v, flip):
    return v + flip - 2 * flip * ((v // flip) % 2)


def remote(src, dst, send, recv, device):
    return pltpu.make_async_remote_copy(
        src_ref=src, dst_ref=dst, send_sem=send, recv_sem=recv, device_id=device, device_id_type=MESH
    )


BEGIN, SHARES_AT = 3.3, 1.0
NEAR_PER, NEAR_DELAY, HOP_PER, HOP_DELAY = 6e-6, 1.1, 5.5e-05, 3.8
FINISH_LAG = 0.5
COSTS = {"number_step": 0.15, "share_forward": 0.08, "subtract": 0.15, "finish": 0.45, "advance": 0.85, "match": 2e-4}


def whole_kernel(
    nv, nr, science_in, basis_in, coeffs_in, row_starts_in, row_taps_in, offsets, col_starts_in, col_taps_in,
    weights, masks_in, decor_in,
    cleaned, template,
    science, basis, coeffs, row_starts, row_taps, col_starts, col_taps, masks, decor, load_sems,
    shares, share_landed, share_sums, numbers, number_landed, number_sums, gathered, warped,
    near_top, near_bottom, packs, pairs_top, pairs_bottom, edges_out, edges_in, borders,
    square, bands, flat, both, second_flat, second_both,
    high, low, second_high, second_low, partial, shifted, mover,
    share_sems, number_sems, halo_sems, late_sems, border_sems,
):
    v, r = lax.axis_index("visit"), lax.axis_index("row")
    rows, columns = science.shape
    width = columns // nv
    parity = v % 2
    turns = flips(nv)
    devices = [(across(v, 1), r)]
    for n in range(1, len(turns)):
        ahead, back = across(v, turns[n]), across(v, turns[len(turns) - n])
        devices.append((ahead + parity * (back - ahead), r))
    chunks = packs.shape[1]
    span = columns // chunks
    part = columns // SUM_PARTS
    half = part // 2
    joined = SUM_PARTS // SHARE_PARTS
    padded = padded_width(columns)
    depth, group = high.shape[0], 3
    second_depth, second_group = second_high.shape[0], 4
    middle = rows + 2 * TAPS

    greet(nv, nr)
    loads = [
        pltpu.make_async_copy(src, dst, load_sems.at[n])
        for n, (src, dst) in enumerate([
            (science_in, science), (col_starts_in, col_starts),
            (masks_in, masks), (coeffs_in, coeffs), (basis_in, basis), (row_starts_in, row_starts),
            (row_taps_in, row_taps), (decor_in, decor), (col_taps_in, col_taps),
        ])
    ]
    for load in loads:
        load.start()
    loads[0].wait()
    quarter = span // 4
    for n in range(chunks):
        for q in range(4):
            at = n * span + q * quarter
            packs[0, n, 2 * q : 2 * q + 2, :] = science[16:18, at : at + quarter]
            packs[1, n, 2 * q : 2 * q + 2, :] = science[rows - 18 : rows - 16, at : at + quarter]
    greeted(nv, nr)
    up, down = [], []
    for n in range(chunks):
        cols = slice(n * span, (n + 1) * span)
        up.append(remote(science.at[0:16, cols], near_bottom.at[:, cols], halo_sems.at[0, n], halo_sems.at[1, n], (v, r - 1)))
        up.append(remote(packs.at[0, n], pairs_bottom.at[n], halo_sems.at[2, n], halo_sems.at[3, n], (v, r - 1)))
        down.append(remote(science.at[rows - 16 : rows, cols], near_top.at[:, cols], halo_sems.at[4, n], halo_sems.at[5, n], (v, r + 1)))
        down.append(remote(packs.at[1, n], pairs_top.at[n], halo_sems.at[6, n], halo_sems.at[7, n], (v, r + 1)))

    @pl.when(r > 0)
    def _():
        for copy in up:
            copy.start()

    @pl.when(r < nr - 1)
    def _():
        for copy in down:
            copy.start()

    for load in loads[1:]:
        load.wait()
    dither = offsets[0]

    def place_of(c):
        return c // joined, slice((c % joined) * half, (c % joined + 1) * half)

    def share_copy(step, w):
        src = shares.at[1 - parity, w] if step == 0 else share_sums.at[step - 1, w]
        return remote(src, share_landed.at[step, w], share_sems.at[0, step, w], share_sems.at[1, step, w], devices[step])

    for w in range(SHARE_PARTS):
        for c in range(w * joined, (w + 1) * joined):
            for h in range(2):
                at = c * part + h * half
                cols = slice(at, at + half)
                start = col_starts[:, cols] + (lax.broadcasted_iota(jnp.int32, (1, half), 1) + (at - dither))
                covered = jnp.where((start >= 0) & (start <= columns - TAPS), weights[0], 0.0)
                shares[h, w, :, place_of(c)[1]] = masks[:, cols].astype(F32) * covered
        share_copy(0, w).start()

    @pl.when(r == 0)
    def _():
        near_top[...] = jnp.zeros_like(near_top)
        pairs_top[...] = jnp.zeros_like(pairs_top)
        edges_in[0] = jnp.zeros_like(edges_in[0])
        borders[0] = jnp.zeros_like(borders[0])

    @pl.when(r == nr - 1)
    def _():
        near_bottom[...] = jnp.zeros_like(near_bottom)
        pairs_bottom[...] = jnp.zeros_like(pairs_bottom)
        edges_in[1] = jnp.zeros_like(edges_in[1])
        borders[1] = jnp.zeros_like(borders[1])

    kernel = coeffs[0] * basis[0]
    for b in range(1, basis.shape[0]):
        kernel = kernel + coeffs[b] * basis[b]
    kernel_t = kernel_transposed(kernel, square)
    m = lax.broadcasted_iota(jnp.int32, (middle, rows), 0) - TAPS
    i = lax.broadcasted_iota(jnp.int32, (middle, rows), 1)
    tap = m - i - row_starts[...]
    inside = (m + r * rows >= 0) & (m + r * rows < nr * rows)
    mix = jnp.zeros((middle, rows), F32)
    for t in range(TAPS):
        mix = mix + jnp.where((tap == t) & inside, row_taps[t : t + 1, :], 0.0)
    for c in range(KS):
        bands[:, c * 128 : (c + 1) * 128] = toeplitz(kernel_t, c, middle, 6)
    folded = lax.dot_general(
        mix, bands[...], (((0,), (0,)), ((), ())), precision=lax.Precision.HIGHEST, preferred_element_type=F32
    )
    flat[...] = jnp.zeros_like(flat)
    for c in range(KS):
        a, b = c // group, c % group
        flat[a * rows : (a + 1) * rows, b * depth : (b + 1) * depth] = folded[:, c * 128 : c * 128 + depth]
    store_both(both, flat[...])

    summed, subtracted, finished = set(), set(), set()

    def share_step(step, w):
        share_copy(step, w).wait()
        before = shares[parity, w] if step == 0 else share_sums[step - 1, w]
        share_sums[step, w] = before + share_landed[step, w]
        summed.add((step, w))
        if step + 1 < len(turns):
            share_copy(step + 1, w).start()

    for w in range(SHARE_PARTS):
        share_step(0, w)

    kernel_t = kernel_transposed(decor[:, 0, :], square)
    second_flat[...] = jnp.zeros_like(second_flat)
    for c in range(KS):
        band = toeplitz(kernel_t, c, rows, 6)
        a, b = c // second_group, c % second_group
        here = slice(a * rows, (a + 1) * rows)
        second_flat[here, b * second_depth : (b + 1) * second_depth] = band[:, 0:second_depth]
    store_both(second_both, second_flat[...])

    for frame in (high, low, second_high, second_low):
        frame[...] = jnp.zeros_like(frame)
    shifted[...] = jnp.zeros_like(shifted)

    tiles = jnp.full((rows, CHUNK + 384), dither // 128, jnp.int32)
    place = lax.broadcasted_iota(jnp.int32, (256, 128), 0) - lax.broadcasted_iota(jnp.int32, (256, 128), 1)
    mover[...] = jnp.where(place == 128 - dither % 128, 1.0, 0.0).astype(BF16)

    def warp(u):
        start = u * CHUNK
        count = CHUNK // 128 + 2
        window = shifted[:, start + 384 : start + 768 + CHUNK]
        for t in range(1, 4):
            at = start + 384 - 128 * t
            window = jnp.where(tiles == t, shifted[:, at : at + CHUNK + 384], window)
        h, l = split(window)
        stack_h = jnp.concatenate([h[:, 128 * j : 128 * j + 256] for j in range(count)], axis=0)
        stack_l = jnp.concatenate([l[:, 128 * j : 128 * j + 256] for j in range(count)], axis=0)
        moved = jnp.dot(stack_h, mover[...], preferred_element_type=F32)
        moved = moved + jnp.dot(stack_l, mover[...], preferred_element_type=F32)
        window = jnp.concatenate([moved[j * rows : (j + 1) * rows] for j in range(count)], axis=1)
        cols = slice(start, start + CHUNK)
        early = col_starts[:, cols] == -3
        taps = [col_taps[t : t + 1, cols] for t in range(TAPS)]
        total = jnp.zeros((rows, CHUNK), F32)
        for lag in range(TAPS + 1):
            now = taps[lag] if lag < TAPS else jnp.zeros_like(taps[0])
            before = taps[lag - 1] if lag > 0 else jnp.zeros_like(taps[0])
            at = 128 + lag - 3
            total = total + jnp.where(early, now, before) * window[:, at : at + CHUNK]
        warped[:, cols] = total
        for n in range(CHUNK // half):
            c, h = (start // half + n) // 2, (start // half + n) % 2
            w, at = place_of(c)
            numbers[c, h] = shares[h, w, :, at] * total[:, n * half : (n + 1) * half]

    last = len(turns)

    def number_copy(step, c):
        sems = number_sems.at[0, step, c], number_sems.at[1, step, c]
        if step == last:
            return remote(gathered.at[c, parity], gathered.at[c, parity], *sems, devices[0])
        src = numbers.at[c, 1 - parity] if step == 0 else number_sums.at[step - 1, c]
        return remote(src, number_landed.at[step, c], *sems, devices[step])

    def late_copies(c):
        return (
            remote(edges_out.at[0, c], edges_in.at[1, c], late_sems.at[0, c], late_sems.at[1, c], (v, r - 1)),
            remote(edges_out.at[1, c], edges_in.at[0, c], late_sems.at[2, c], late_sems.at[3, c], (v, r + 1)),
        )

    def border_copies(c, up):
        if c < SUM_PARTS - BORDER_PARTS:
            return []
        n = c - SUM_PARTS + BORDER_PARTS
        side, row, src = (1, r - 1, slice(0, 16)) if up else (0, r + 1, slice(rows - 16, rows))
        return [
            remote(
                gathered.at[c, parity, src], borders.at[side, n, parity],
                border_sems.at[0, side, k, n], border_sems.at[1, side, k, n], (column, row),
            )
            for k, column in enumerate((v, across(v, 1)))
        ]

    def apart(c):
        return c >= SUM_PARTS - BORDER_PARTS

    def outward(c, values, h):
        here = slice(h * half, (h + 1) * half)
        edges_out[0, c, :, here] = values[0:8]
        edges_out[1, c, :, here] = values[rows - 8 : rows]
        for q in range(2):
            cut = slice(q * (half // 2), (q + 1) * (half // 2))
            k = 4 * h + 2 * q
            edges_out[0, c, k : k + 2, part : part + half // 2] = values[8:10, cut]
            edges_out[1, c, k : k + 2, part : part + half // 2] = values[rows - 10 : rows - 8, cut]
        if h == 0:
            return
        to_above, to_below = late_copies(c)

        @pl.when(r > 0)
        def _():
            to_above.start()

        @pl.when(r < nr - 1)
        def _():
            to_below.start()

    queue, clock, free = [], BEGIN, {}
    done = {"pieces": 0, "sums": 0, "warps": 0, "parts": 0, "second": 0, "outs": 0}
    starts = [n * CHUNK for n in range(-(-padded // CHUNK))]
    ends = [min(at + CHUNK, padded) for at in starts]
    bounds = [0] + [at + PAD for at in starts[1 : columns // CHUNK]] + [columns]
    order = iter(range(1 << 20))

    def later(link, elements, action, lag=0.0):
        per, delay = (NEAR_PER, NEAR_DELAY) if link == 0 else (HOP_PER, HOP_DELAY)
        per = 7.2e-5 if link == "row" else per
        free[link] = max(clock, free.get(link, 0.0)) + per * elements
        heapq.heappush(queue, (free[link] + delay + lag, next(order), action))

    def number_step(step, c):
        number_copy(step, c).wait()
        before = numbers[c, parity] if step == 0 else number_sums[step - 1, c]
        total = before + number_landed[step, c]
        if step + 1 < last:
            number_sums[step, c] = total
            number_copy(step + 1, c).start()
            later(step + 1, rows * half, functools.partial(number_step, step + 1, c))
            return
        w, at = place_of(c)
        assert (last - 1, w) in summed
        gathered[c, parity] = total / jnp.maximum(share_sums[last - 1, w, :, at], 1.0)
        number_copy(last, c).start()
        if apart(c):

            @pl.when(r > 0)
            def _():
                for copy in border_copies(c, True):
                    copy.start()

            @pl.when(r < nr - 1)
            def _():
                for copy in border_copies(c, False):
                    copy.start()

        later(0, rows * half, functools.partial(subtract, c))
        if apart(c):
            later("row", 32 * half, functools.partial(finish, c), FINISH_LAG)

    def subtract(c):
        number_copy(last, c).wait()
        for h in range(2):
            at = c * part + h * half
            cols = slice(at, at + half)
            values = warped[:, cols] - gathered[c, h]
            hi, lo = split(values)
            second_high[16 : 16 + rows, PAD + at : PAD + at + half] = hi
            second_low[16 : 16 + rows, PAD + at : PAD + at + half] = lo
            if not apart(c):
                outward(c, values, h)
        subtracted.add(c)
        if not apart(c):
            later("row", 10 * part, functools.partial(finish, c), FINISH_LAG)

    def finish(c):
        assert c in subtracted
        to_above, to_below = late_copies(c)

        @pl.when(r > 0)
        def _():
            to_below.wait_recv()
            for copy in border_copies(c, False):
                copy.wait_recv()

        @pl.when(r < nr - 1)
        def _():
            to_above.wait_recv()
            for copy in border_copies(c, True):
                copy.wait_recv()

        frames = second_high, second_low
        for h in range(2):
            here = slice(h * half, (h + 1) * half)
            at = PAD + c * part + h * half
            top, bottom = edges_in[0, c, :, here], edges_in[1, c, :, here]
            n = c - SUM_PARTS + BORDER_PARTS
            if apart(c):
                top, bottom = top - borders[0, n, h, 8:16], bottom - borders[1, n, h, 0:8]
            store_split(*frames, 8, at, top)
            store_split(*frames, 16 + rows, at, bottom)
            for q in range(2):
                cut = slice(q * (half // 2), (q + 1) * (half // 2))
                k, wide = 4 * h + 2 * q, slice(part, part + half // 2)
                top, bottom = edges_in[0, c, k : k + 2, wide], edges_in[1, c, k : k + 2, wide]
                if apart(c):
                    top, bottom = top - borders[0, n, h, 6:8, cut], bottom - borders[1, n, h, 8:10, cut]
                store_split(*frames, 6, at + q * (half // 2), top)
                store_split(*frames, 24 + rows, at + q * (half // 2), bottom)
        finished.add(c)
        known = next((n for n in range(SUM_PARTS) if n not in finished), SUM_PARTS)
        while done["second"] < len(starts) and (known == SUM_PARTS or ends[done["second"]] + 8 - PAD <= known * part):
            n = done["second"]
            piece(second_high, second_low, second_both, partial, starts[n], ends[n], second_group)
            done["second"] += 1
            if n > 0:
                cleaned[:, starts[n - 1] : starts[n]] = shifted_sum(partial, starts[n - 1], starts[n], rows, second_group)

    def match(n):
        cols = slice(n * span, (n + 1) * span)

        @pl.when(r > 0)
        def _():
            down[2 * n].wait_recv()
            down[2 * n + 1].wait_recv()

        @pl.when(r < nr - 1)
        def _():
            up[2 * n].wait_recv()
            up[2 * n + 1].wait_recv()

        store_split(high, low, 24, PAD + n * span, science[:, cols])
        store_split(high, low, 8, PAD + n * span, near_top[:, cols])
        store_split(high, low, 24 + rows, PAD + n * span, near_bottom[:, cols])
        for q in range(4):
            at = PAD + n * span + q * quarter
            store_split(high, low, 6, at, pairs_top[n, 2 * q : 2 * q + 2, :])
            store_split(high, low, 40 + rows, at, pairs_bottom[n, 2 * q : 2 * q + 2, :])

    def advance(ready):
        n = done["pieces"]
        if n < len(starts) and enough(ready):
            piece(high, low, both, partial, starts[n], ends[n], group)
            done["pieces"] += 1
            return True
        return False

    def enough(ready):
        n = done["pieces"]
        return n >= len(starts) or ready == columns or ends[n] + group - PAD <= ready

    def warps():
        while done["sums"] < columns // CHUNK and done["sums"] + 2 <= done["pieces"]:
            start, end = bounds[done["sums"] : done["sums"] + 2]
            shifted[:, 640 + start : 640 + end] = shifted_sum(partial, start, end, rows, group)
            done["sums"] += 1
        while done["warps"] < columns // CHUNK and (
            bounds[done["sums"]] >= (done["warps"] + 1) * CHUNK + 8 or bounds[done["sums"]] == columns
        ):
            warp(done["warps"])
            done["warps"] += 1
        while (done["parts"] + 1) * part <= done["warps"] * CHUNK:
            number_copy(0, done["parts"]).start()
            for h in range(2 if apart(done["parts"]) else 0):
                at = done["parts"] * part + h * half
                outward(done["parts"], warped[:, at : at + half], h)
            later(0, rows * half, functools.partial(number_step, 0, done["parts"]))
            done["parts"] += 1

    def share_forward(step, w):
        share_step(step, w)
        if step + 1 < last:
            later(step + 1, rows * half * joined, functools.partial(share_forward, step + 1, w))

    for w in range(SHARE_PARTS):
        clock = SHARES_AT
        later(1, rows * half * joined, functools.partial(share_forward, 1, w))
    clock = BEGIN
    landed = [HOP_DELAY + (n + 1) * span * 18 * HOP_PER for n in range(chunks)]
    arrived = 0
    while queue or done["warps"] < columns // CHUNK:
        working = done["warps"] < columns // CHUNK
        ready = clock
        if working and arrived < chunks and not enough(arrived * span):
            ready = max(clock, landed[arrived])
        if queue and (not working or queue[0][0] <= ready):
            at, _, action = heapq.heappop(queue)
            clock = max(clock, at)
            action()
            clock += COSTS[action.func.__name__]
            continue
        clock = ready
        if advance(arrived * span):
            clock += COSTS["advance"]
            warps()
        else:
            match(arrived)
            arrived += 1
            clock += COSTS["match"] * span

    if half <= width:
        for k in range(width // half):
            n = v * (width // half) + k
            template[:, k * half : (k + 1) * half] = gathered[n // 2, n % 2]
    else:
        n = v * width // half
        template[...] = gathered[n // 2, n % 2, :, pl.ds(pl.multiple_of((v * width) % half, width), width)]

    for c in range(SUM_PARTS):
        to_above, to_below = late_copies(c)

        @pl.when(r > 0)
        def _():
            for copy in [to_above] + border_copies(c, True):
                copy.wait_send()

        @pl.when(r < nr - 1)
        def _():
            for copy in [to_below] + border_copies(c, False):
                copy.wait_send()

    @pl.when(r > 0)
    def _():
        for copy in up:
            copy.wait_send()

    @pl.when(r < nr - 1)
    def _():
        for copy in down:
            copy.wait_send()


def hand_over(cleaned, template, cleaned_out, template_out, sems):
    first = pltpu.make_async_copy(cleaned, cleaned_out, sems.at[0])
    second = pltpu.make_async_copy(template, template_out, sems.at[1])
    first.start()
    second.start()
    first.wait()
    second.wait()


def shape(*dims):
    return jax.ShapeDtypeStruct(dims, F32)


def in_hbm(array):
    return pltpu.with_memory_space_constraint(array, pltpu.HBM)


def on_device(
    nv, nr, science, basis_kernels, basis_coeffs, row_starts, row_taps, col_offsets,
    col_starts, col_taps, visit_weights, clip_masks, decorrelation,
):
    pixels = science[0]
    rows, columns = pixels.shape
    width = columns // nv
    padded = padded_width(columns)
    depth, group = 80, 3
    tall = -(-KS // group) * rows
    second_depth, second_group = rows + 32, 4
    wide = -(-KS // second_group) * rows
    part, span = columns // SUM_PARTS, columns // HALO_PARTS
    half, share_half, turns = part // 2, columns // SHARE_PARTS // 2, len(flips(nv))
    f32 = lambda *dims: pltpu.VMEM(dims, F32)
    bf16 = lambda *dims: pltpu.VMEM(dims, BF16)
    cleaned, template = pl.pallas_call(
        functools.partial(whole_kernel, nv, nr),
        out_shape=(pltpu.VMEM((rows, columns), F32), pltpu.VMEM((rows, width), F32)),
        in_specs=[HBM] * 5 + [SMEM] + [HBM] * 2 + [SMEM] + [HBM] * 2,
        out_specs=(VMEM, VMEM),
        scratch_shapes=[
            f32(rows, columns), f32(*basis_kernels.shape), pltpu.SMEM(basis_coeffs.shape[1:], F32),
            pltpu.VMEM((1, rows), jnp.int32), f32(TAPS, rows),
            pltpu.VMEM((1, columns), jnp.int32), f32(TAPS, columns),
            pltpu.VMEM((rows, columns), jnp.int32), f32(KS, 1, KS), pltpu.SemaphoreType.DMA((9,)),
            f32(2, SHARE_PARTS, rows, share_half), f32(turns, SHARE_PARTS, rows, share_half),
            f32(turns, SHARE_PARTS, rows, share_half),
            f32(SUM_PARTS, 2, rows, half), f32(turns, SUM_PARTS, rows, half), f32(turns - 1, SUM_PARTS, rows, half),
            f32(SUM_PARTS, 2, rows, half), f32(rows, columns),
            f32(16, columns), f32(16, columns), f32(2, HALO_PARTS, 8, span // 4),
            f32(HALO_PARTS, 8, span // 4), f32(HALO_PARTS, 8, span // 4),
            f32(2, SUM_PARTS, 8, part + half // 2), f32(2, SUM_PARTS, 8, part + half // 2),
            f32(2, BORDER_PARTS, 2, 16, half),
            f32(128, 128), f32(rows + 2 * TAPS, KS * 128),
            f32(tall, group * depth), bf16(2 * tall, group * depth),
            f32(wide, second_group * second_depth), bf16(2 * wide, second_group * second_depth),
            bf16(depth, padded + 128), bf16(depth, padded + 128),
            bf16(second_depth, padded + 128), bf16(second_depth, padded + 128),
            f32(tall, padded), f32(rows, columns + 1024), bf16(256, 128),
            pltpu.SemaphoreType.DMA((2, turns, SHARE_PARTS)),
            pltpu.SemaphoreType.DMA((2, turns + 1, SUM_PARTS)),
            pltpu.SemaphoreType.DMA((8, HALO_PARTS)),
            pltpu.SemaphoreType.DMA((4, SUM_PARTS)),
            pltpu.SemaphoreType.DMA((2, 2, 2, BORDER_PARTS)),
        ],
        compiler_params=pltpu.CompilerParams(
            collective_id=0, has_side_effects=True, vmem_limit_bytes=28 * 1024 * 1024
        ),
        name="whole",
    )(
        *map(in_hbm, (pixels, basis_kernels, basis_coeffs[0], row_starts, row_taps[0])), col_offsets,
        *map(in_hbm, (col_starts, col_taps[0])), visit_weights,
        *map(in_hbm, (clip_masks[0], jnp.transpose(decorrelation, (1, 0, 2)))),
    )
    cleaned, template = pl.pallas_call(
        hand_over,
        out_shape=(shape(rows, columns), shape(rows, width)),
        in_specs=[VMEM, VMEM],
        out_specs=(HBM, HBM),
        scratch_shapes=[pltpu.SemaphoreType.DMA((2,))],
        compiler_params=pltpu.CompilerParams(vmem_limit_bytes=8 * 1024 * 1024),
        name="hand_over",
    )(cleaned, template)
    return (cleaned[None], template)


def solution(mesh):
    nv, nr = mesh.shape["visit"], mesh.shape["row"]
    return jax.shard_map(
        functools.partial(on_device, nv, nr),
        mesh=mesh,
        in_specs=(
            P("visit", "row", None),
            P(),
            P("visit", None),
            P("visit", "row"),
            P("visit", None, "row"),
            P("visit"),
            P("visit", None),
            P("visit", None, None),
            P("visit"),
            P("visit", "row", None),
            P("visit", None, None),
        ),
        out_specs=(P("visit", "row", None), P("row", "visit")),
        check_vma=False,
    )
```

```python
import functools
import heapq

import jax
import jax.numpy as jnp
from jax import lax
from jax.experimental import pallas as pl
from jax.experimental.pallas import tpu as pltpu
from jax.sharding import PartitionSpec as P

KS = 21
HALF = KS // 2
TAPS = 8
PAD = 128
CHUNK = 512
HALO_PARTS = 8
SUM_PARTS = 8
SHARE_PARTS = 4
BORDER_PARTS = 3
F32 = jnp.float32
BF16 = jnp.bfloat16
MESH = pl.DeviceIdType.MESH
VMEM = pl.BlockSpec(memory_space=pltpu.VMEM)
HBM = pl.BlockSpec(memory_space=pltpu.HBM)
SMEM = pl.BlockSpec(memory_space=pltpu.SMEM)


def padded_width(columns):
    return -(-(columns + 2 * PAD) // PAD) * PAD


def split(x):
    high = x.astype(BF16)
    low = (x - high.astype(F32)).astype(BF16)
    return high, low


def toeplitz(kernel_t, c, rows, lead):
    line = jnp.broadcast_to(kernel_t[c : c + 1, :], (rows, 128))
    return pltpu.roll(line, lead, 1, stride=1, stride_axis=0)


def kernel_transposed(kernel, square):
    square[...] = jnp.zeros_like(square)
    square[0:KS, 0:KS] = kernel
    return jnp.transpose(square[...])


def piece(high, low, both, partial, start, end, group):
    m, wide = both.shape[0] // 2, end - start
    window_h = high[:, start : end + 128]
    window_l = low[:, start : end + 128]
    stack_h = jnp.concatenate([window_h[:, b : b + wide] for b in range(group)], axis=0)
    stack_l = jnp.concatenate([window_l[:, b : b + wide] for b in range(group)], axis=0)
    top = jnp.dot(both[...], stack_h, preferred_element_type=F32)
    rest = jnp.dot(both[0:m, :], stack_l, preferred_element_type=F32)
    partial[0:m, start:end] = top[0:m] + (top[m : 2 * m] + rest)


def shifted_sum(partial, start, end, rows, group):
    total = jnp.zeros((rows, end - start), F32)
    for a in range(-(-KS // group)):
        window = partial[a * rows : (a + 1) * rows, start : end + 2 * PAD]
        shift = PAD + group * a - HALF
        total = total + window[:, shift : shift + end - start]
    return total


def store_split(high, low, row, column, values):
    h, l = split(values)
    high[row : row + values.shape[0], column : column + values.shape[1]] = h
    low[row : row + values.shape[0], column : column + values.shape[1]] = l


def store_both(both, values):
    h, l = split(values)
    m = values.shape[0]
    both[0:m, :] = h
    both[m : 2 * m, :] = l


def flips(nv):
    return [1 << bit for bit in range(nv.bit_length() - 1)]


def greet(nv, nr):
    v, r = lax.axis_index("visit"), lax.axis_index("row")
    barrier = pltpu.get_barrier_semaphore()

    def hello(a, b):
        pl.semaphore_signal(barrier, inc=1, device_id=(a, b), device_id_type=MESH)

    for flip in flips(nv):
        hello(across(v, flip), r)

    @pl.when(r > 0)
    def _():
        hello(v, r - 1)
        hello(across(v, 1), r - 1)

    @pl.when(r < nr - 1)
    def _():
        hello(v, r + 1)
        hello(across(v, 1), r + 1)


def greeted(nv, nr):
    r = lax.axis_index("row")
    above, below = (r > 0).astype(jnp.int32), (r < nr - 1).astype(jnp.int32)
    pl.semaphore_wait(pltpu.get_barrier_semaphore(), len(flips(nv)) + 2 * above + 2 * below)


def across(v, flip):
    return v + flip - 2 * flip * ((v // flip) % 2)


def remote(src, dst, send, recv, device):
    return pltpu.make_async_remote_copy(
        src_ref=src, dst_ref=dst, send_sem=send, recv_sem=recv, device_id=device, device_id_type=MESH
    )


BEGIN, SHARES_AT = 3.3, 1.0
NEAR_PER, NEAR_DELAY, HOP_PER, HOP_DELAY = 6e-6, 1.0, 5.5e-05, 4.3
FINISH_LAG = 0.5
COSTS = {"number_step": 0.15, "share_forward": 0.08, "subtract": 0.15, "finish": 0.6, "advance": 0.85, "match": 2e-4}


def whole_kernel(
    nv, nr, science_in, basis_in, coeffs_in, row_starts_in, row_taps_in, offsets, col_starts_in, col_taps_in,
    weights, masks_in, decor_in,
    cleaned, template,
    science, basis, coeffs, row_starts, row_taps, col_starts, col_taps, masks, decor, load_sems,
    shares, share_landed, share_sums, numbers, number_landed, number_sums, gathered, warped,
    near_top, near_bottom, packs, pairs_top, pairs_bottom, edges_out, edges_in, borders,
    square, bands, flat, both, second_flat, second_both,
    high, low, second_high, second_low, partial, shifted, mover,
    share_sems, number_sems, halo_sems, late_sems, border_sems,
):
    v, r = lax.axis_index("visit"), lax.axis_index("row")
    rows, columns = science.shape
    width = columns // nv
    parity = v % 2
    turns = flips(nv)
    devices = [(across(v, 1), r)]
    for n in range(1, len(turns)):
        ahead, back = across(v, turns[n]), across(v, turns[len(turns) - n])
        devices.append((ahead + parity * (back - ahead), r))
    chunks = packs.shape[1]
    span = columns // chunks
    part = columns // SUM_PARTS
    half = part // 2
    joined = SUM_PARTS // SHARE_PARTS
    padded = padded_width(columns)
    depth, group = high.shape[0], 3
    second_depth, second_group = second_high.shape[0], 4
    middle = rows + 2 * TAPS

    greet(nv, nr)
    loads = [
        pltpu.make_async_copy(src, dst, load_sems.at[n])
        for n, (src, dst) in enumerate([
            (science_in, science), (col_starts_in, col_starts),
            (masks_in, masks), (coeffs_in, coeffs), (basis_in, basis), (row_starts_in, row_starts),
            (row_taps_in, row_taps), (decor_in, decor), (col_taps_in, col_taps),
        ])
    ]
    for load in loads:
        load.start()
    loads[0].wait()
    quarter = span // 4
    for n in range(chunks):
        for q in range(4):
            at = n * span + q * quarter
            packs[0, n, 2 * q : 2 * q + 2, :] = science[16:18, at : at + quarter]
            packs[1, n, 2 * q : 2 * q + 2, :] = science[rows - 18 : rows - 16, at : at + quarter]
    greeted(nv, nr)
    up, down = [], []
    for n in range(chunks):
        cols = slice(n * span, (n + 1) * span)
        up.append(remote(science.at[0:16, cols], near_bottom.at[:, cols], halo_sems.at[0, n], halo_sems.at[1, n], (v, r - 1)))
        up.append(remote(packs.at[0, n], pairs_bottom.at[n], halo_sems.at[2, n], halo_sems.at[3, n], (v, r - 1)))
        down.append(remote(science.at[rows - 16 : rows, cols], near_top.at[:, cols], halo_sems.at[4, n], halo_sems.at[5, n], (v, r + 1)))
        down.append(remote(packs.at[1, n], pairs_top.at[n], halo_sems.at[6, n], halo_sems.at[7, n], (v, r + 1)))

    @pl.when(r > 0)
    def _():
        for copy in up:
            copy.start()

    @pl.when(r < nr - 1)
    def _():
        for copy in down:
            copy.start()

    for load in loads[1:]:
        load.wait()
    dither = offsets[0]

    def place_of(c):
        return c // joined, slice((c % joined) * half, (c % joined + 1) * half)

    def share_copy(step, w):
        src = shares.at[1 - parity, w] if step == 0 else share_sums.at[step - 1, w]
        return remote(src, share_landed.at[step, w], share_sems.at[0, step, w], share_sems.at[1, step, w], devices[step])

    for w in range(SHARE_PARTS):
        for c in range(w * joined, (w + 1) * joined):
            for h in range(2):
                at = c * part + h * half
                cols = slice(at, at + half)
                start = col_starts[:, cols] + (lax.broadcasted_iota(jnp.int32, (1, half), 1) + (at - dither))
                covered = jnp.where((start >= 0) & (start <= columns - TAPS), weights[0], 0.0)
                shares[h, w, :, place_of(c)[1]] = masks[:, cols].astype(F32) * covered
        share_copy(0, w).start()

    @pl.when(r == 0)
    def _():
        near_top[...] = jnp.zeros_like(near_top)
        pairs_top[...] = jnp.zeros_like(pairs_top)
        edges_in[0] = jnp.zeros_like(edges_in[0])
        borders[0] = jnp.zeros_like(borders[0])

    @pl.when(r == nr - 1)
    def _():
        near_bottom[...] = jnp.zeros_like(near_bottom)
        pairs_bottom[...] = jnp.zeros_like(pairs_bottom)
        edges_in[1] = jnp.zeros_like(edges_in[1])
        borders[1] = jnp.zeros_like(borders[1])

    kernel = coeffs[0] * basis[0]
    for b in range(1, basis.shape[0]):
        kernel = kernel + coeffs[b] * basis[b]
    kernel_t = kernel_transposed(kernel, square)
    m = lax.broadcasted_iota(jnp.int32, (middle, rows), 0) - TAPS
    i = lax.broadcasted_iota(jnp.int32, (middle, rows), 1)
    tap = m - i - row_starts[...]
    inside = (m + r * rows >= 0) & (m + r * rows < nr * rows)
    mix = jnp.zeros((middle, rows), F32)
    for t in range(TAPS):
        mix = mix + jnp.where((tap == t) & inside, row_taps[t : t + 1, :], 0.0)
    for c in range(KS):
        bands[:, c * 128 : (c + 1) * 128] = toeplitz(kernel_t, c, middle, 6)
    summed, subtracted, finished = set(), set(), set()

    def share_step(step, w):
        share_copy(step, w).wait()
        before = shares[parity, w] if step == 0 else share_sums[step - 1, w]
        share_sums[step, w] = before + share_landed[step, w]
        summed.add((step, w))
        if step + 1 < len(turns):
            share_copy(step + 1, w).start()

    for w in range(SHARE_PARTS):
        share_step(0, w)

    folded = lax.dot_general(
        mix, bands[...], (((0,), (0,)), ((), ())), precision=lax.Precision.HIGHEST, preferred_element_type=F32
    )
    flat[...] = jnp.zeros_like(flat)
    for c in range(KS):
        a, b = c // group, c % group
        flat[a * rows : (a + 1) * rows, b * depth : (b + 1) * depth] = folded[:, c * 128 : c * 128 + depth]
    store_both(both, flat[...])

    kernel_t = kernel_transposed(decor[:, 0, :], square)
    second_flat[...] = jnp.zeros_like(second_flat)
    for c in range(KS):
        band = toeplitz(kernel_t, c, rows, 6)
        a, b = c // second_group, c % second_group
        here = slice(a * rows, (a + 1) * rows)
        second_flat[here, b * second_depth : (b + 1) * second_depth] = band[:, 0:second_depth]
    store_both(second_both, second_flat[...])

    for frame in (high, low, second_high, second_low):
        frame[...] = jnp.zeros_like(frame)
    shifted[...] = jnp.zeros_like(shifted)

    tiles = jnp.full((rows, CHUNK + 384), dither // 128, jnp.int32)
    place = lax.broadcasted_iota(jnp.int32, (256, 128), 0) - lax.broadcasted_iota(jnp.int32, (256, 128), 1)
    mover[...] = jnp.where(place == 128 - dither % 128, 1.0, 0.0).astype(BF16)

    def warp(u):
        start = u * CHUNK
        count = CHUNK // 128 + 2
        window = shifted[:, start + 384 : start + 768 + CHUNK]
        for t in range(1, 4):
            at = start + 384 - 128 * t
            window = jnp.where(tiles == t, shifted[:, at : at + CHUNK + 384], window)
        h, l = split(window)
        stack_h = jnp.concatenate([h[:, 128 * j : 128 * j + 256] for j in range(count)], axis=0)
        stack_l = jnp.concatenate([l[:, 128 * j : 128 * j + 256] for j in range(count)], axis=0)
        moved = jnp.dot(stack_h, mover[...], preferred_element_type=F32)
        moved = moved + jnp.dot(stack_l, mover[...], preferred_element_type=F32)
        window = jnp.concatenate([moved[j * rows : (j + 1) * rows] for j in range(count)], axis=1)
        cols = slice(start, start + CHUNK)
        early = col_starts[:, cols] == -3
        taps = [col_taps[t : t + 1, cols] for t in range(TAPS)]
        total = jnp.zeros((rows, CHUNK), F32)
        for lag in range(TAPS + 1):
            now = taps[lag] if lag < TAPS else jnp.zeros_like(taps[0])
            before = taps[lag - 1] if lag > 0 else jnp.zeros_like(taps[0])
            at = 128 + lag - 3
            total = total + jnp.where(early, now, before) * window[:, at : at + CHUNK]
        warped[:, cols] = total
        for n in range(CHUNK // half):
            c, h = (start // half + n) // 2, (start // half + n) % 2
            w, at = place_of(c)
            numbers[c, h] = shares[h, w, :, at] * total[:, n * half : (n + 1) * half]

    last = len(turns)

    def number_copy(step, c):
        sems = number_sems.at[0, step, c], number_sems.at[1, step, c]
        if step == last:
            return remote(gathered.at[c, parity], gathered.at[c, parity], *sems, devices[0])
        src = numbers.at[c, 1 - parity] if step == 0 else number_sums.at[step - 1, c]
        return remote(src, number_landed.at[step, c], *sems, devices[step])

    def late_copies(c):
        return (
            remote(edges_out.at[0, c], edges_in.at[1, c], late_sems.at[0, c], late_sems.at[1, c], (v, r - 1)),
            remote(edges_out.at[1, c], edges_in.at[0, c], late_sems.at[2, c], late_sems.at[3, c], (v, r + 1)),
        )

    def border_copies(c, up):
        if c < SUM_PARTS - BORDER_PARTS:
            return []
        n = c - SUM_PARTS + BORDER_PARTS
        side, row, src = (1, r - 1, slice(0, 16)) if up else (0, r + 1, slice(rows - 16, rows))
        return [
            remote(
                gathered.at[c, parity, src], borders.at[side, n, parity],
                border_sems.at[0, side, k, n], border_sems.at[1, side, k, n], (column, row),
            )
            for k, column in enumerate((v, across(v, 1)))
        ]

    def apart(c):
        return c >= SUM_PARTS - BORDER_PARTS

    def outward(c, values, h):
        here = slice(h * half, (h + 1) * half)
        edges_out[0, c, :, here] = values[0:8]
        edges_out[1, c, :, here] = values[rows - 8 : rows]
        for q in range(2):
            cut = slice(q * (half // 2), (q + 1) * (half // 2))
            k = 4 * h + 2 * q
            edges_out[0, c, k : k + 2, part : part + half // 2] = values[8:10, cut]
            edges_out[1, c, k : k + 2, part : part + half // 2] = values[rows - 10 : rows - 8, cut]
        if h == 0:
            return
        to_above, to_below = late_copies(c)

        @pl.when(r > 0)
        def _():
            to_above.start()

        @pl.when(r < nr - 1)
        def _():
            to_below.start()

    queue, clock, free = [], BEGIN, {}
    done = {"pieces": 0, "sums": 0, "warps": 0, "parts": 0, "second": 0, "outs": 0}
    starts = [n * CHUNK for n in range(-(-padded // CHUNK))]
    ends = [min(at + CHUNK, padded) for at in starts]
    bounds = [0] + [at + PAD for at in starts[1 : columns // CHUNK]] + [columns]
    order = iter(range(1 << 20))

    def later(link, elements, action, lag=0.0):
        per, delay = (NEAR_PER, NEAR_DELAY) if link == 0 else (HOP_PER, HOP_DELAY)
        per = 7.2e-5 if link == "row" else per
        free[link] = max(clock, free.get(link, 0.0)) + per * elements
        heapq.heappush(queue, (free[link] + delay + lag, next(order), action))

    def number_step(step, c):
        number_copy(step, c).wait()
        before = numbers[c, parity] if step == 0 else number_sums[step - 1, c]
        total = before + number_landed[step, c]
        if step + 1 < last:
            number_sums[step, c] = total
            number_copy(step + 1, c).start()
            later(step + 1, rows * half, functools.partial(number_step, step + 1, c))
            return
        w, at = place_of(c)
        assert (last - 1, w) in summed
        gathered[c, parity] = total / jnp.maximum(share_sums[last - 1, w, :, at], 1.0)
        number_copy(last, c).start()
        if apart(c):

            @pl.when(r > 0)
            def _():
                for copy in border_copies(c, True):
                    copy.start()

            @pl.when(r < nr - 1)
            def _():
                for copy in border_copies(c, False):
                    copy.start()

        later(0, rows * half, functools.partial(subtract, c))
        if apart(c):
            later("row", 32 * half, functools.partial(finish, c), FINISH_LAG)

    def subtract(c):
        number_copy(last, c).wait()
        for h in range(2):
            at = c * part + h * half
            cols = slice(at, at + half)
            values = warped[:, cols] - gathered[c, h]
            hi, lo = split(values)
            second_high[16 : 16 + rows, PAD + at : PAD + at + half] = hi
            second_low[16 : 16 + rows, PAD + at : PAD + at + half] = lo
            if not apart(c):
                outward(c, values, h)
        subtracted.add(c)
        if not apart(c):
            later("row", 10 * part, functools.partial(finish, c), FINISH_LAG)

    def finish(c):
        assert c in subtracted
        to_above, to_below = late_copies(c)

        @pl.when(r > 0)
        def _():
            to_below.wait_recv()
            for copy in border_copies(c, False):
                copy.wait_recv()

        @pl.when(r < nr - 1)
        def _():
            to_above.wait_recv()
            for copy in border_copies(c, True):
                copy.wait_recv()

        frames = second_high, second_low
        for h in range(2):
            here = slice(h * half, (h + 1) * half)
            at = PAD + c * part + h * half
            top, bottom = edges_in[0, c, :, here], edges_in[1, c, :, here]
            n = c - SUM_PARTS + BORDER_PARTS
            if apart(c):
                top, bottom = top - borders[0, n, h, 8:16], bottom - borders[1, n, h, 0:8]
            store_split(*frames, 8, at, top)
            store_split(*frames, 16 + rows, at, bottom)
            for q in range(2):
                cut = slice(q * (half // 2), (q + 1) * (half // 2))
                k, wide = 4 * h + 2 * q, slice(part, part + half // 2)
                top, bottom = edges_in[0, c, k : k + 2, wide], edges_in[1, c, k : k + 2, wide]
                if apart(c):
                    top, bottom = top - borders[0, n, h, 6:8, cut], bottom - borders[1, n, h, 8:10, cut]
                store_split(*frames, 6, at + q * (half // 2), top)
                store_split(*frames, 24 + rows, at + q * (half // 2), bottom)
        finished.add(c)
        known = next((n for n in range(SUM_PARTS) if n not in finished), SUM_PARTS)
        while done["second"] < len(starts) and (known == SUM_PARTS or ends[done["second"]] + 8 - PAD <= known * part):
            n = done["second"]
            piece(second_high, second_low, second_both, partial, starts[n], ends[n], second_group)
            done["second"] += 1
            if n > 0:
                cleaned[:, starts[n - 1] : starts[n]] = shifted_sum(partial, starts[n - 1], starts[n], rows, second_group)

    def match(n):
        cols = slice(n * span, (n + 1) * span)

        @pl.when(r > 0)
        def _():
            down[2 * n].wait_recv()
            down[2 * n + 1].wait_recv()

        @pl.when(r < nr - 1)
        def _():
            up[2 * n].wait_recv()
            up[2 * n + 1].wait_recv()

        store_split(high, low, 24, PAD + n * span, science[:, cols])
        store_split(high, low, 8, PAD + n * span, near_top[:, cols])
        store_split(high, low, 24 + rows, PAD + n * span, near_bottom[:, cols])
        for q in range(4):
            at = PAD + n * span + q * quarter
            store_split(high, low, 6, at, pairs_top[n, 2 * q : 2 * q + 2, :])
            store_split(high, low, 40 + rows, at, pairs_bottom[n, 2 * q : 2 * q + 2, :])

    def advance(ready):
        n = done["pieces"]
        if n < len(starts) and enough(ready):
            piece(high, low, both, partial, starts[n], ends[n], group)
            done["pieces"] += 1
            return True
        return False

    def enough(ready):
        n = done["pieces"]
        return n >= len(starts) or ready == columns or ends[n] + group - PAD <= ready

    def warps():
        while done["sums"] < columns // CHUNK and done["sums"] + 2 <= done["pieces"]:
            start, end = bounds[done["sums"] : done["sums"] + 2]
            shifted[:, 640 + start : 640 + end] = shifted_sum(partial, start, end, rows, group)
            done["sums"] += 1
        while done["warps"] < columns // CHUNK and (
            bounds[done["sums"]] >= (done["warps"] + 1) * CHUNK + 8 or bounds[done["sums"]] == columns
        ):
            warp(done["warps"])
            done["warps"] += 1
        while (done["parts"] + 1) * part <= done["warps"] * CHUNK:
            number_copy(0, done["parts"]).start()
            for h in range(2 if apart(done["parts"]) else 0):
                at = done["parts"] * part + h * half
                outward(done["parts"], warped[:, at : at + half], h)
            later(0, rows * half, functools.partial(number_step, 0, done["parts"]))
            done["parts"] += 1

    def share_forward(step, w):
        share_step(step, w)
        if step + 1 < last:
            later(step + 1, rows * half * joined, functools.partial(share_forward, step + 1, w))

    for w in range(SHARE_PARTS):
        clock = SHARES_AT
        later(1, rows * half * joined, functools.partial(share_forward, 1, w))
    clock = BEGIN
    landed = [HOP_DELAY + (n + 1) * span * 18 * HOP_PER for n in range(chunks)]
    arrived = 0
    while queue or done["warps"] < columns // CHUNK:
        working = done["warps"] < columns // CHUNK
        ready = clock
        if working and arrived < chunks and not enough(arrived * span):
            ready = max(clock, landed[arrived])
        if queue and (not working or queue[0][0] <= ready):
            at, _, action = heapq.heappop(queue)
            clock = max(clock, at)
            action()
            clock += COSTS[action.func.__name__]
            continue
        clock = ready
        if advance(arrived * span):
            clock += COSTS["advance"]
            warps()
        else:
            match(arrived)
            arrived += 1
            clock += COSTS["match"] * span

    if half <= width:
        for k in range(width // half):
            n = v * (width // half) + k
            template[:, k * half : (k + 1) * half] = gathered[n // 2, n % 2]
    else:
        n = v * width // half
        template[...] = gathered[n // 2, n % 2, :, pl.ds(pl.multiple_of((v * width) % half, width), width)]

    for c in range(SUM_PARTS):
        to_above, to_below = late_copies(c)

        @pl.when(r > 0)
        def _():
            for copy in [to_above] + border_copies(c, True):
                copy.wait_send()

        @pl.when(r < nr - 1)
        def _():
            for copy in [to_below] + border_copies(c, False):
                copy.wait_send()

    @pl.when(r > 0)
    def _():
        for copy in up:
            copy.wait_send()

    @pl.when(r < nr - 1)
    def _():
        for copy in down:
            copy.wait_send()


def hand_over(cleaned, template, cleaned_out, template_out, sems):
    first = pltpu.make_async_copy(cleaned, cleaned_out, sems.at[0])
    second = pltpu.make_async_copy(template, template_out, sems.at[1])
    first.start()
    second.start()
    first.wait()
    second.wait()


def shape(*dims):
    return jax.ShapeDtypeStruct(dims, F32)


def in_hbm(array):
    return pltpu.with_memory_space_constraint(array, pltpu.HBM)


def on_device(
    nv, nr, science, basis_kernels, basis_coeffs, row_starts, row_taps, col_offsets,
    col_starts, col_taps, visit_weights, clip_masks, decorrelation,
):
    pixels = science[0]
    rows, columns = pixels.shape
    width = columns // nv
    padded = padded_width(columns)
    depth, group = 80, 3
    tall = -(-KS // group) * rows
    second_depth, second_group = rows + 32, 4
    wide = -(-KS // second_group) * rows
    part, span = columns // SUM_PARTS, columns // HALO_PARTS
    half, share_half, turns = part // 2, columns // SHARE_PARTS // 2, len(flips(nv))
    f32 = lambda *dims: pltpu.VMEM(dims, F32)
    bf16 = lambda *dims: pltpu.VMEM(dims, BF16)
    cleaned, template = pl.pallas_call(
        functools.partial(whole_kernel, nv, nr),
        out_shape=(pltpu.VMEM((rows, columns), F32), pltpu.VMEM((rows, width), F32)),
        in_specs=[HBM] * 5 + [SMEM] + [HBM] * 2 + [SMEM] + [HBM] * 2,
        out_specs=(VMEM, VMEM),
        scratch_shapes=[
            f32(rows, columns), f32(*basis_kernels.shape), pltpu.SMEM(basis_coeffs.shape[1:], F32),
            pltpu.VMEM((1, rows), jnp.int32), f32(TAPS, rows),
            pltpu.VMEM((1, columns), jnp.int32), f32(TAPS, columns),
            pltpu.VMEM((rows, columns), jnp.int32), f32(KS, 1, KS), pltpu.SemaphoreType.DMA((9,)),
            f32(2, SHARE_PARTS, rows, share_half), f32(turns, SHARE_PARTS, rows, share_half),
            f32(turns, SHARE_PARTS, rows, share_half),
            f32(SUM_PARTS, 2, rows, half), f32(turns, SUM_PARTS, rows, half), f32(turns - 1, SUM_PARTS, rows, half),
            f32(SUM_PARTS, 2, rows, half), f32(rows, columns),
            f32(16, columns), f32(16, columns), f32(2, HALO_PARTS, 8, span // 4),
            f32(HALO_PARTS, 8, span // 4), f32(HALO_PARTS, 8, span // 4),
            f32(2, SUM_PARTS, 8, part + half // 2), f32(2, SUM_PARTS, 8, part + half // 2),
            f32(2, BORDER_PARTS, 2, 16, half),
            f32(128, 128), f32(rows + 2 * TAPS, KS * 128),
            f32(tall, group * depth), bf16(2 * tall, group * depth),
            f32(wide, second_group * second_depth), bf16(2 * wide, second_group * second_depth),
            bf16(depth, padded + 128), bf16(depth, padded + 128),
            bf16(second_depth, padded + 128), bf16(second_depth, padded + 128),
            f32(tall, padded), f32(rows, columns + 1024), bf16(256, 128),
            pltpu.SemaphoreType.DMA((2, turns, SHARE_PARTS)),
            pltpu.SemaphoreType.DMA((2, turns + 1, SUM_PARTS)),
            pltpu.SemaphoreType.DMA((8, HALO_PARTS)),
            pltpu.SemaphoreType.DMA((4, SUM_PARTS)),
            pltpu.SemaphoreType.DMA((2, 2, 2, BORDER_PARTS)),
        ],
        compiler_params=pltpu.CompilerParams(
            collective_id=0, has_side_effects=True, vmem_limit_bytes=28 * 1024 * 1024
        ),
        name="whole",
    )(
        *map(in_hbm, (pixels, basis_kernels, basis_coeffs[0], row_starts, row_taps[0])), col_offsets,
        *map(in_hbm, (col_starts, col_taps[0])), visit_weights,
        *map(in_hbm, (clip_masks[0], jnp.transpose(decorrelation, (1, 0, 2)))),
    )
    cleaned, template = pl.pallas_call(
        hand_over,
        out_shape=(shape(rows, columns), shape(rows, width)),
        in_specs=[VMEM, VMEM],
        out_specs=(HBM, HBM),
        scratch_shapes=[pltpu.SemaphoreType.DMA((2,))],
        compiler_params=pltpu.CompilerParams(vmem_limit_bytes=8 * 1024 * 1024),
        name="hand_over",
    )(cleaned, template)
    return (cleaned[None], template)


def solution(mesh):
    nv, nr = mesh.shape["visit"], mesh.shape["row"]
    return jax.shard_map(
        functools.partial(on_device, nv, nr),
        mesh=mesh,
        in_specs=(
            P("visit", "row", None),
            P(),
            P("visit", None),
            P("visit", "row"),
            P("visit", None, "row"),
            P("visit"),
            P("visit", None),
            P("visit", None, None),
            P("visit"),
            P("visit", "row", None),
            P("visit", None, None),
        ),
        out_specs=(P("visit", "row", None), P("row", "visit")),
        check_vma=False,
    )
```

```python
import functools
import heapq

import jax
import jax.numpy as jnp
from jax import lax
from jax.experimental import pallas as pl
from jax.experimental.pallas import tpu as pltpu
from jax.sharding import PartitionSpec as P

KS = 21
HALF = KS // 2
TAPS = 8
PAD = 128
CHUNK = 512
HALO_PARTS = 8
SUM_PARTS = 8
SHARE_PARTS = 4
BORDER_PARTS = 3
F32 = jnp.float32
BF16 = jnp.bfloat16
MESH = pl.DeviceIdType.MESH
VMEM = pl.BlockSpec(memory_space=pltpu.VMEM)
HBM = pl.BlockSpec(memory_space=pltpu.HBM)
SMEM = pl.BlockSpec(memory_space=pltpu.SMEM)


def padded_width(columns):
    return -(-(columns + 2 * PAD) // PAD) * PAD


def split(x):
    high = x.astype(BF16)
    low = (x - high.astype(F32)).astype(BF16)
    return high, low


def toeplitz(kernel_t, c, rows, lead):
    line = jnp.broadcast_to(kernel_t[c : c + 1, :], (rows, 128))
    return pltpu.roll(line, lead, 1, stride=1, stride_axis=0)


def kernel_transposed(kernel, square):
    square[...] = jnp.zeros_like(square)
    square[0:KS, 0:KS] = kernel
    return jnp.transpose(square[...])


def piece(high, low, both, partial, start, end, group):
    m, wide = both.shape[0] // 2, end - start
    window_h = high[:, start : end + 128]
    window_l = low[:, start : end + 128]
    stack_h = jnp.concatenate([window_h[:, b : b + wide] for b in range(group)], axis=0)
    stack_l = jnp.concatenate([window_l[:, b : b + wide] for b in range(group)], axis=0)
    top = jnp.dot(both[...], stack_h, preferred_element_type=F32)
    rest = jnp.dot(both[0:m, :], stack_l, preferred_element_type=F32)
    partial[0:m, start:end] = top[0:m] + (top[m : 2 * m] + rest)


def shifted_sum(partial, start, end, rows, group):
    total = jnp.zeros((rows, end - start), F32)
    for a in range(-(-KS // group)):
        window = partial[a * rows : (a + 1) * rows, start : end + 2 * PAD]
        shift = PAD + group * a - HALF
        total = total + window[:, shift : shift + end - start]
    return total


def store_split(high, low, row, column, values):
    h, l = split(values)
    high[row : row + values.shape[0], column : column + values.shape[1]] = h
    low[row : row + values.shape[0], column : column + values.shape[1]] = l


def store_both(both, values):
    h, l = split(values)
    m = values.shape[0]
    both[0:m, :] = h
    both[m : 2 * m, :] = l


def flips(nv):
    return [1 << bit for bit in range(nv.bit_length() - 1)]


def greet(nv, nr):
    v, r = lax.axis_index("visit"), lax.axis_index("row")
    barrier = pltpu.get_barrier_semaphore()

    def hello(a, b):
        pl.semaphore_signal(barrier, inc=1, device_id=(a, b), device_id_type=MESH)

    for flip in flips(nv):
        hello(across(v, flip), r)

    @pl.when(r > 0)
    def _():
        hello(v, r - 1)
        hello(across(v, 1), r - 1)

    @pl.when(r < nr - 1)
    def _():
        hello(v, r + 1)
        hello(across(v, 1), r + 1)


def greeted(nv, nr):
    r = lax.axis_index("row")
    above, below = (r > 0).astype(jnp.int32), (r < nr - 1).astype(jnp.int32)
    pl.semaphore_wait(pltpu.get_barrier_semaphore(), len(flips(nv)) + 2 * above + 2 * below)


def across(v, flip):
    return v + flip - 2 * flip * ((v // flip) % 2)


def remote(src, dst, send, recv, device):
    return pltpu.make_async_remote_copy(
        src_ref=src, dst_ref=dst, send_sem=send, recv_sem=recv, device_id=device, device_id_type=MESH
    )


BEGIN, SHARES_AT = 3.3, 1.0
NEAR_PER, NEAR_DELAY, HOP_PER, HOP_DELAY = 6e-6, 1.1, 5.5e-05, 3.8
FINISH_LAG = 0.5
COSTS = {"number_step": 0.15, "share_forward": 0.08, "subtract": 0.15, "finish": 0.6, "advance": 0.8, "match": 2e-4}


def whole_kernel(
    nv, nr, science_in, basis_in, coeffs_in, row_starts_in, row_taps_in, offsets, col_starts_in, col_taps_in,
    weights, masks_in, decor_in,
    cleaned, template,
    science, basis, coeffs, row_starts, row_taps, col_starts, col_taps, masks, decor, load_sems,
    shares, share_landed, share_sums, numbers, number_landed, number_sums, gathered, warped,
    near_top, near_bottom, packs, pairs_top, pairs_bottom, edges_out, edges_in, borders,
    square, bands, flat, both, second_flat, second_both,
    high, low, second_high, second_low, partial, shifted, mover,
    share_sems, number_sems, halo_sems, late_sems, border_sems,
):
    v, r = lax.axis_index("visit"), lax.axis_index("row")
    rows, columns = science.shape
    width = columns // nv
    parity = v % 2
    turns = flips(nv)
    devices = [(across(v, 1), r)]
    for n in range(1, len(turns)):
        ahead, back = across(v, turns[n]), across(v, turns[len(turns) - n])
        devices.append((ahead + parity * (back - ahead), r))
    chunks = packs.shape[1]
    span = columns // chunks
    part = columns // SUM_PARTS
    half = part // 2
    joined = SUM_PARTS // SHARE_PARTS
    padded = padded_width(columns)
    depth, group = high.shape[0], 3
    second_depth, second_group = second_high.shape[0], 4
    middle = rows + 2 * TAPS

    greet(nv, nr)
    loads = [
        pltpu.make_async_copy(src, dst, load_sems.at[n])
        for n, (src, dst) in enumerate([
            (science_in, science), (col_starts_in, col_starts),
            (masks_in, masks), (coeffs_in, coeffs), (basis_in, basis), (row_starts_in, row_starts),
            (row_taps_in, row_taps), (decor_in, decor), (col_taps_in, col_taps),
        ])
    ]
    for load in loads:
        load.start()
    loads[0].wait()
    quarter = span // 4
    for n in range(chunks):
        for q in range(4):
            at = n * span + q * quarter
            packs[0, n, 2 * q : 2 * q + 2, :] = science[16:18, at : at + quarter]
            packs[1, n, 2 * q : 2 * q + 2, :] = science[rows - 18 : rows - 16, at : at + quarter]
    greeted(nv, nr)
    up, down = [], []
    for n in range(chunks):
        cols = slice(n * span, (n + 1) * span)
        up.append(remote(science.at[0:16, cols], near_bottom.at[:, cols], halo_sems.at[0, n], halo_sems.at[1, n], (v, r - 1)))
        up.append(remote(packs.at[0, n], pairs_bottom.at[n], halo_sems.at[2, n], halo_sems.at[3, n], (v, r - 1)))
        down.append(remote(science.at[rows - 16 : rows, cols], near_top.at[:, cols], halo_sems.at[4, n], halo_sems.at[5, n], (v, r + 1)))
        down.append(remote(packs.at[1, n], pairs_top.at[n], halo_sems.at[6, n], halo_sems.at[7, n], (v, r + 1)))

    @pl.when(r > 0)
    def _():
        for copy in up:
            copy.start()

    @pl.when(r < nr - 1)
    def _():
        for copy in down:
            copy.start()

    for load in loads[1:]:
        load.wait()
    dither = offsets[0]

    def place_of(c):
        return c // joined, slice((c % joined) * half, (c % joined + 1) * half)

    def share_copy(step, w):
        src = shares.at[1 - parity, w] if step == 0 else share_sums.at[step - 1, w]
        return remote(src, share_landed.at[step, w], share_sems.at[0, step, w], share_sems.at[1, step, w], devices[step])

    for w in range(SHARE_PARTS):
        for c in range(w * joined, (w + 1) * joined):
            for h in range(2):
                at = c * part + h * half
                cols = slice(at, at + half)
                start = col_starts[:, cols] + (lax.broadcasted_iota(jnp.int32, (1, half), 1) + (at - dither))
                covered = jnp.where((start >= 0) & (start <= columns - TAPS), weights[0], 0.0)
                shares[h, w, :, place_of(c)[1]] = masks[:, cols].astype(F32) * covered
        share_copy(0, w).start()

    @pl.when(r == 0)
    def _():
        near_top[...] = jnp.zeros_like(near_top)
        pairs_top[...] = jnp.zeros_like(pairs_top)
        edges_in[0] = jnp.zeros_like(edges_in[0])
        borders[0] = jnp.zeros_like(borders[0])

    @pl.when(r == nr - 1)
    def _():
        near_bottom[...] = jnp.zeros_like(near_bottom)
        pairs_bottom[...] = jnp.zeros_like(pairs_bottom)
        edges_in[1] = jnp.zeros_like(edges_in[1])
        borders[1] = jnp.zeros_like(borders[1])

    kernel = coeffs[0] * basis[0]
    for b in range(1, basis.shape[0]):
        kernel = kernel + coeffs[b] * basis[b]
    kernel_t = kernel_transposed(kernel, square)
    m = lax.broadcasted_iota(jnp.int32, (middle, rows), 0) - TAPS
    i = lax.broadcasted_iota(jnp.int32, (middle, rows), 1)
    tap = m - i - row_starts[...]
    inside = (m + r * rows >= 0) & (m + r * rows < nr * rows)
    mix = jnp.zeros((middle, rows), F32)
    for t in range(TAPS):
        mix = mix + jnp.where((tap == t) & inside, row_taps[t : t + 1, :], 0.0)
    for c in range(KS):
        bands[:, c * 128 : (c + 1) * 128] = toeplitz(kernel_t, c, middle, 6)
    summed, subtracted, finished = set(), set(), set()

    def share_step(step, w):
        share_copy(step, w).wait()
        before = shares[parity, w] if step == 0 else share_sums[step - 1, w]
        share_sums[step, w] = before + share_landed[step, w]
        summed.add((step, w))
        if step + 1 < len(turns):
            share_copy(step + 1, w).start()

    for w in range(SHARE_PARTS):
        share_step(0, w)

    folded = lax.dot_general(
        mix, bands[...], (((0,), (0,)), ((), ())), precision=lax.Precision.HIGHEST, preferred_element_type=F32
    )
    flat[...] = jnp.zeros_like(flat)
    for c in range(KS):
        a, b = c // group, c % group
        flat[a * rows : (a + 1) * rows, b * depth : (b + 1) * depth] = folded[:, c * 128 : c * 128 + depth]
    store_both(both, flat[...])

    kernel_t = kernel_transposed(decor[:, 0, :], square)
    second_flat[...] = jnp.zeros_like(second_flat)
    for c in range(KS):
        band = toeplitz(kernel_t, c, rows, 6)
        a, b = c // second_group, c % second_group
        here = slice(a * rows, (a + 1) * rows)
        second_flat[here, b * second_depth : (b + 1) * second_depth] = band[:, 0:second_depth]
    store_both(second_both, second_flat[...])

    for frame in (high, low, second_high, second_low):
        frame[...] = jnp.zeros_like(frame)
    shifted[...] = jnp.zeros_like(shifted)

    tiles = jnp.full((rows, CHUNK + 384), dither // 128, jnp.int32)
    place = lax.broadcasted_iota(jnp.int32, (256, 128), 0) - lax.broadcasted_iota(jnp.int32, (256, 128), 1)
    mover[...] = jnp.where(place == 128 - dither % 128, 1.0, 0.0).astype(BF16)

    def warp(u):
        start = u * CHUNK
        count = CHUNK // 128 + 2
        window = shifted[:, start + 384 : start + 768 + CHUNK]
        for t in range(1, 4):
            at = start + 384 - 128 * t
            window = jnp.where(tiles == t, shifted[:, at : at + CHUNK + 384], window)
        h, l = split(window)
        stack_h = jnp.concatenate([h[:, 128 * j : 128 * j + 256] for j in range(count)], axis=0)
        stack_l = jnp.concatenate([l[:, 128 * j : 128 * j + 256] for j in range(count)], axis=0)
        moved = jnp.dot(stack_h, mover[...], preferred_element_type=F32)
        moved = moved + jnp.dot(stack_l, mover[...], preferred_element_type=F32)
        window = jnp.concatenate([moved[j * rows : (j + 1) * rows] for j in range(count)], axis=1)
        cols = slice(start, start + CHUNK)
        early = col_starts[:, cols] == -3
        taps = [col_taps[t : t + 1, cols] for t in range(TAPS)]
        total = jnp.zeros((rows, CHUNK), F32)
        for lag in range(TAPS + 1):
            now = taps[lag] if lag < TAPS else jnp.zeros_like(taps[0])
            before = taps[lag - 1] if lag > 0 else jnp.zeros_like(taps[0])
            at = 128 + lag - 3
            total = total + jnp.where(early, now, before) * window[:, at : at + CHUNK]
        warped[:, cols] = total
        for n in range(CHUNK // half):
            c, h = (start // half + n) // 2, (start // half + n) % 2
            w, at = place_of(c)
            numbers[c, h] = shares[h, w, :, at] * total[:, n * half : (n + 1) * half]

    last = len(turns)

    def number_copy(step, c):
        sems = number_sems.at[0, step, c], number_sems.at[1, step, c]
        if step == last:
            return remote(gathered.at[c, parity], gathered.at[c, parity], *sems, devices[0])
        src = numbers.at[c, 1 - parity] if step == 0 else number_sums.at[step - 1, c]
        return remote(src, number_landed.at[step, c], *sems, devices[step])

    def late_copies(c):
        return (
            remote(edges_out.at[0, c], edges_in.at[1, c], late_sems.at[0, c], late_sems.at[1, c], (v, r - 1)),
            remote(edges_out.at[1, c], edges_in.at[0, c], late_sems.at[2, c], late_sems.at[3, c], (v, r + 1)),
        )

    def border_copies(c, up):
        if c < SUM_PARTS - BORDER_PARTS:
            return []
        n = c - SUM_PARTS + BORDER_PARTS
        side, row, src = (1, r - 1, slice(0, 16)) if up else (0, r + 1, slice(rows - 16, rows))
        return [
            remote(
                gathered.at[c, parity, src], borders.at[side, n, parity],
                border_sems.at[0, side, k, n], border_sems.at[1, side, k, n], (column, row),
            )
            for k, column in enumerate((v, across(v, 1)))
        ]

    def apart(c):
        return c >= SUM_PARTS - BORDER_PARTS

    def outward(c, values, h):
        here = slice(h * half, (h + 1) * half)
        edges_out[0, c, :, here] = values[0:8]
        edges_out[1, c, :, here] = values[rows - 8 : rows]
        for q in range(2):
            cut = slice(q * (half // 2), (q + 1) * (half // 2))
            k = 4 * h + 2 * q
            edges_out[0, c, k : k + 2, part : part + half // 2] = values[8:10, cut]
            edges_out[1, c, k : k + 2, part : part + half // 2] = values[rows - 10 : rows - 8, cut]
        if h == 0:
            return
        to_above, to_below = late_copies(c)

        @pl.when(r > 0)
        def _():
            to_above.start()

        @pl.when(r < nr - 1)
        def _():
            to_below.start()

    queue, clock, free = [], BEGIN, {}
    done = {"pieces": 0, "sums": 0, "warps": 0, "parts": 0, "second": 0, "outs": 0}
    starts = [n * CHUNK for n in range(-(-padded // CHUNK))]
    ends = [min(at + CHUNK, padded) for at in starts]
    bounds = [0] + [at + PAD for at in starts[1 : columns // CHUNK]] + [columns]
    order = iter(range(1 << 20))

    def later(link, elements, action, lag=0.0):
        per, delay = (NEAR_PER, NEAR_DELAY) if link == 0 else (HOP_PER, HOP_DELAY)
        per = 7.2e-5 if link == "row" else per
        free[link] = max(clock, free.get(link, 0.0)) + per * elements
        heapq.heappush(queue, (free[link] + delay + lag, next(order), action))

    def number_step(step, c):
        number_copy(step, c).wait()
        before = numbers[c, parity] if step == 0 else number_sums[step - 1, c]
        total = before + number_landed[step, c]
        if step + 1 < last:
            number_sums[step, c] = total
            number_copy(step + 1, c).start()
            later(step + 1, rows * half, functools.partial(number_step, step + 1, c))
            return
        w, at = place_of(c)
        assert (last - 1, w) in summed
        gathered[c, parity] = total / jnp.maximum(share_sums[last - 1, w, :, at], 1.0)
        number_copy(last, c).start()
        if apart(c):

            @pl.when(r > 0)
            def _():
                for copy in border_copies(c, True):
                    copy.start()

            @pl.when(r < nr - 1)
            def _():
                for copy in border_copies(c, False):
                    copy.start()

        later(0, rows * half, functools.partial(subtract, c))
        if apart(c):
            later("row", 32 * half, functools.partial(finish, c), FINISH_LAG)

    def subtract(c):
        number_copy(last, c).wait()
        for h in range(2):
            at = c * part + h * half
            cols = slice(at, at + half)
            values = warped[:, cols] - gathered[c, h]
            hi, lo = split(values)
            second_high[16 : 16 + rows, PAD + at : PAD + at + half] = hi
            second_low[16 : 16 + rows, PAD + at : PAD + at + half] = lo
            if not apart(c):
                outward(c, values, h)
        subtracted.add(c)
        if not apart(c):
            later("row", 10 * part, functools.partial(finish, c), FINISH_LAG)

    def finish(c):
        assert c in subtracted
        to_above, to_below = late_copies(c)

        @pl.when(r > 0)
        def _():
            to_below.wait_recv()
            for copy in border_copies(c, False):
                copy.wait_recv()

        @pl.when(r < nr - 1)
        def _():
            to_above.wait_recv()
            for copy in border_copies(c, True):
                copy.wait_recv()

        frames = second_high, second_low
        for h in range(2):
            here = slice(h * half, (h + 1) * half)
            at = PAD + c * part + h * half
            top, bottom = edges_in[0, c, :, here], edges_in[1, c, :, here]
            n = c - SUM_PARTS + BORDER_PARTS
            if apart(c):
                top, bottom = top - borders[0, n, h, 8:16], bottom - borders[1, n, h, 0:8]
            store_split(*frames, 8, at, top)
            store_split(*frames, 16 + rows, at, bottom)
            for q in range(2):
                cut = slice(q * (half // 2), (q + 1) * (half // 2))
                k, wide = 4 * h + 2 * q, slice(part, part + half // 2)
                top, bottom = edges_in[0, c, k : k + 2, wide], edges_in[1, c, k : k + 2, wide]
                if apart(c):
                    top, bottom = top - borders[0, n, h, 6:8, cut], bottom - borders[1, n, h, 8:10, cut]
                store_split(*frames, 6, at + q * (half // 2), top)
                store_split(*frames, 24 + rows, at + q * (half // 2), bottom)
        finished.add(c)
        known = next((n for n in range(SUM_PARTS) if n not in finished), SUM_PARTS)
        while done["second"] < len(starts) and (known == SUM_PARTS or ends[done["second"]] + 8 - PAD <= known * part):
            n = done["second"]
            piece(second_high, second_low, second_both, partial, starts[n], ends[n], second_group)
            done["second"] += 1
            if n > 0:
                cleaned[:, starts[n - 1] : starts[n]] = shifted_sum(partial, starts[n - 1], starts[n], rows, second_group)

    def match(n):
        cols = slice(n * span, (n + 1) * span)

        @pl.when(r > 0)
        def _():
            down[2 * n].wait_recv()
            down[2 * n + 1].wait_recv()

        @pl.when(r < nr - 1)
        def _():
            up[2 * n].wait_recv()
            up[2 * n + 1].wait_recv()

        store_split(high, low, 24, PAD + n * span, science[:, cols])
        store_split(high, low, 8, PAD + n * span, near_top[:, cols])
        store_split(high, low, 24 + rows, PAD + n * span, near_bottom[:, cols])
        for q in range(4):
            at = PAD + n * span + q * quarter
            store_split(high, low, 6, at, pairs_top[n, 2 * q : 2 * q + 2, :])
            store_split(high, low, 40 + rows, at, pairs_bottom[n, 2 * q : 2 * q + 2, :])

    def advance(ready):
        n = done["pieces"]
        if n < len(starts) and enough(ready):
            piece(high, low, both, partial, starts[n], ends[n], group)
            done["pieces"] += 1
            return True
        return False

    def enough(ready):
        n = done["pieces"]
        return n >= len(starts) or ready == columns or ends[n] + group - PAD <= ready

    def warps():
        while done["sums"] < columns // CHUNK and done["sums"] + 2 <= done["pieces"]:
            start, end = bounds[done["sums"] : done["sums"] + 2]
            shifted[:, 640 + start : 640 + end] = shifted_sum(partial, start, end, rows, group)
            done["sums"] += 1
        while done["warps"] < columns // CHUNK and (
            bounds[done["sums"]] >= (done["warps"] + 1) * CHUNK + 8 or bounds[done["sums"]] == columns
        ):
            warp(done["warps"])
            done["warps"] += 1
        while (done["parts"] + 1) * part <= done["warps"] * CHUNK:
            number_copy(0, done["parts"]).start()
            for h in range(2 if apart(done["parts"]) else 0):
                at = done["parts"] * part + h * half
                outward(done["parts"], warped[:, at : at + half], h)
            later(0, rows * half, functools.partial(number_step, 0, done["parts"]))
            done["parts"] += 1

    def share_forward(step, w):
        share_step(step, w)
        if step + 1 < last:
            later(step + 1, rows * half * joined, functools.partial(share_forward, step + 1, w))

    for w in range(SHARE_PARTS):
        clock = SHARES_AT
        later(1, rows * half * joined, functools.partial(share_forward, 1, w))
    clock = BEGIN
    landed = [HOP_DELAY + (n + 1) * span * 18 * HOP_PER for n in range(chunks)]
    arrived = 0
    while queue or done["warps"] < columns // CHUNK:
        working = done["warps"] < columns // CHUNK
        ready = clock
        if working and arrived < chunks and not enough(arrived * span):
            ready = max(clock, landed[arrived])
        if queue and (not working or queue[0][0] <= ready):
            at, _, action = heapq.heappop(queue)
            clock = max(clock, at)
            action()
            clock += COSTS[action.func.__name__]
            continue
        clock = ready
        if advance(arrived * span):
            clock += COSTS["advance"]
            warps()
        else:
            match(arrived)
            arrived += 1
            clock += COSTS["match"] * span

    if half <= width:
        for k in range(width // half):
            n = v * (width // half) + k
            template[:, k * half : (k + 1) * half] = gathered[n // 2, n % 2]
    else:
        n = v * width // half
        template[...] = gathered[n // 2, n % 2, :, pl.ds(pl.multiple_of((v * width) % half, width), width)]

    for c in range(SUM_PARTS):
        to_above, to_below = late_copies(c)

        @pl.when(r > 0)
        def _():
            for copy in [to_above] + border_copies(c, True):
                copy.wait_send()

        @pl.when(r < nr - 1)
        def _():
            for copy in [to_below] + border_copies(c, False):
                copy.wait_send()

    @pl.when(r > 0)
    def _():
        for copy in up:
            copy.wait_send()

    @pl.when(r < nr - 1)
    def _():
        for copy in down:
            copy.wait_send()


def hand_over(cleaned, template, cleaned_out, template_out, sems):
    first = pltpu.make_async_copy(cleaned, cleaned_out, sems.at[0])
    second = pltpu.make_async_copy(template, template_out, sems.at[1])
    first.start()
    second.start()
    first.wait()
    second.wait()


def shape(*dims):
    return jax.ShapeDtypeStruct(dims, F32)


def in_hbm(array):
    return pltpu.with_memory_space_constraint(array, pltpu.HBM)


def on_device(
    nv, nr, science, basis_kernels, basis_coeffs, row_starts, row_taps, col_offsets,
    col_starts, col_taps, visit_weights, clip_masks, decorrelation,
):
    pixels = science[0]
    rows, columns = pixels.shape
    width = columns // nv
    padded = padded_width(columns)
    depth, group = 80, 3
    tall = -(-KS // group) * rows
    second_depth, second_group = rows + 32, 4
    wide = -(-KS // second_group) * rows
    part, span = columns // SUM_PARTS, columns // HALO_PARTS
    half, share_half, turns = part // 2, columns // SHARE_PARTS // 2, len(flips(nv))
    f32 = lambda *dims: pltpu.VMEM(dims, F32)
    bf16 = lambda *dims: pltpu.VMEM(dims, BF16)
    cleaned, template = pl.pallas_call(
        functools.partial(whole_kernel, nv, nr),
        out_shape=(pltpu.VMEM((rows, columns), F32), pltpu.VMEM((rows, width), F32)),
        in_specs=[HBM] * 5 + [SMEM] + [HBM] * 2 + [SMEM] + [HBM] * 2,
        out_specs=(VMEM, VMEM),
        scratch_shapes=[
            f32(rows, columns), f32(*basis_kernels.shape), pltpu.SMEM(basis_coeffs.shape[1:], F32),
            pltpu.VMEM((1, rows), jnp.int32), f32(TAPS, rows),
            pltpu.VMEM((1, columns), jnp.int32), f32(TAPS, columns),
            pltpu.VMEM((rows, columns), jnp.int32), f32(KS, 1, KS), pltpu.SemaphoreType.DMA((9,)),
            f32(2, SHARE_PARTS, rows, share_half), f32(turns, SHARE_PARTS, rows, share_half),
            f32(turns, SHARE_PARTS, rows, share_half),
            f32(SUM_PARTS, 2, rows, half), f32(turns, SUM_PARTS, rows, half), f32(turns - 1, SUM_PARTS, rows, half),
            f32(SUM_PARTS, 2, rows, half), f32(rows, columns),
            f32(16, columns), f32(16, columns), f32(2, HALO_PARTS, 8, span // 4),
            f32(HALO_PARTS, 8, span // 4), f32(HALO_PARTS, 8, span // 4),
            f32(2, SUM_PARTS, 8, part + half // 2), f32(2, SUM_PARTS, 8, part + half // 2),
            f32(2, BORDER_PARTS, 2, 16, half),
            f32(128, 128), f32(rows + 2 * TAPS, KS * 128),
            f32(tall, group * depth), bf16(2 * tall, group * depth),
            f32(wide, second_group * second_depth), bf16(2 * wide, second_group * second_depth),
            bf16(depth, padded + 128), bf16(depth, padded + 128),
            bf16(second_depth, padded + 128), bf16(second_depth, padded + 128),
            f32(tall, padded), f32(rows, columns + 1024), bf16(256, 128),
            pltpu.SemaphoreType.DMA((2, turns, SHARE_PARTS)),
            pltpu.SemaphoreType.DMA((2, turns + 1, SUM_PARTS)),
            pltpu.SemaphoreType.DMA((8, HALO_PARTS)),
            pltpu.SemaphoreType.DMA((4, SUM_PARTS)),
            pltpu.SemaphoreType.DMA((2, 2, 2, BORDER_PARTS)),
        ],
        compiler_params=pltpu.CompilerParams(
            collective_id=0, has_side_effects=True, vmem_limit_bytes=28 * 1024 * 1024
        ),
        name="whole",
    )(
        *map(in_hbm, (pixels, basis_kernels, basis_coeffs[0], row_starts, row_taps[0])), col_offsets,
        *map(in_hbm, (col_starts, col_taps[0])), visit_weights,
        *map(in_hbm, (clip_masks[0], jnp.transpose(decorrelation, (1, 0, 2)))),
    )
    cleaned, template = pl.pallas_call(
        hand_over,
        out_shape=(shape(rows, columns), shape(rows, width)),
        in_specs=[VMEM, VMEM],
        out_specs=(HBM, HBM),
        scratch_shapes=[pltpu.SemaphoreType.DMA((2,))],
        compiler_params=pltpu.CompilerParams(vmem_limit_bytes=8 * 1024 * 1024),
        name="hand_over",
    )(cleaned, template)
    return (cleaned[None], template)


def solution(mesh):
    nv, nr = mesh.shape["visit"], mesh.shape["row"]
    return jax.shard_map(
        functools.partial(on_device, nv, nr),
        mesh=mesh,
        in_specs=(
            P("visit", "row", None),
            P(),
            P("visit", None),
            P("visit", "row"),
            P("visit", None, "row"),
            P("visit"),
            P("visit", None),
            P("visit", None, None),
            P("visit"),
            P("visit", "row", None),
            P("visit", None, None),
        ),
        out_specs=(P("visit", "row", None), P("row", "visit")),
        check_vma=False,
    )
```
